1024 devices in a mesh: seq: 16 (over x, y_hi, core), dp: 64 (over y_lo, z).
Axes of the slice: x: 4, y: 8 (y_hi: 2, y_lo: 4; y = y_hi * 4 + y_lo), z: 16, core: 2. Of those that a mesh axis runs over, the one named last changes fastest.
Arguments:
- queries: bfloat16 [64, 2048, 2048], P('dp', 'seq'), may hold values from -6 to 6
- keys: bfloat16 [64, 2048, 2048], P('dp', 'seq'), may hold values from -6 to 6
- values: bfloat16 [64, 2048, 2048], P('dp', 'seq'), may hold values from -6 to 6
- master: float32 [2048, 1024], P(('seq', 'dp')), may hold values from -0.24 to 0.24
- moment: float32 [2048, 1024], P(('seq', 'dp')), may hold values from -0.06 to 0.06
- second: float32 [2048, 1024], P(('seq', 'dp')), may hold values from 1e-06 to 0.0001
- gradient: float32 [2048, 1024], P(('seq', 'dp')), may hold values from -0.18 to 0.18
Outputs:
- projected: bfloat16 [64, 2048, 1024], P('dp', 'seq')
- new_master: float32 [2048, 1024], P(('seq', 'dp'))
The draws below stay inside these ranges and needn't reach their ends.
All inputs are finite; a program needn't handle non-finite values.
Results may differ from the reference program's by a relative error of at most 0.0063.
Values may be sent and summed in bfloat16 or wider, within the bound.
A program may use at most 32 MiB of HBM per device.

```python
import math
import jax
import jax.numpy as jnp
from jax import lax

HEADS = 16
HEAD_DIM = 128
D_OUT = 1024
LENGTH = 2048
SEQS = 64


def drawn(key, which):
    base = jax.random.normal(jax.random.fold_in(key, which), (SEQS, LENGTH, HEADS, HEAD_DIM), jnp.float32)
    base = jnp.clip(base, -6.0, 6.0)
    return base.reshape(SEQS, LENGTH, HEADS * HEAD_DIM).astype(jnp.bfloat16)


def draw_queries(key, part):
    return drawn(key, 1)


def draw_keys(key, part):
    return drawn(key, 2)


def block_levels(rng, extent, split, least, high):
    factor_of = 1.0
    for dim, blocks in split:
        heights = jax.random.uniform(jax.random.fold_in(jax.random.fold_in(rng, 6), dim), (blocks,), jnp.float32, least / len(split), high / len(split))
        factor_of = factor_of * jnp.repeat(jnp.exp(heights), extent[dim] // blocks).reshape((-1,) + (1,) * (len(extent) - 1 - dim))
    return factor_of


def scatter_about(rng, shape, width, limit, cuts=(), kind=jnp.bfloat16):
    factor_of = block_levels(rng, shape, cuts, -0.22, 0.18) if cuts else 1.0
    result = jax.random.normal(rng, shape, jnp.float32) * width * factor_of
    return jnp.minimum(jnp.maximum(result, -limit), limit).astype(kind)


def setup_inputs(seed: int = 0) -> dict:
    key_list = jax.random.split(jax.random.key(seed), 8)
    queries = draw_queries(jax.random.fold_in(key_list[7], 71), 0)
    keys = draw_keys(jax.random.fold_in(key_list[7], 71), 0)
    values = scatter_about(key_list[2], (SEQS, LENGTH, HEADS * HEAD_DIM), 1.0, 6.0, ((0, 64), (1, 16)))
    master = scatter_about(key_list[3], (HEADS * HEAD_DIM, D_OUT), 0.04, 0.24, ((0, 1024),), jnp.float32)
    moment = scatter_about(key_list[4], (HEADS * HEAD_DIM, D_OUT), 0.01, 0.06, ((0, 1024),), jnp.float32)
    second = jnp.clip(jnp.exp(math.log(0.0001) - 4.6051702 * jax.random.uniform(key_list[5], (HEADS * HEAD_DIM, D_OUT), jnp.float32) ** block_levels(key_list[5], (HEADS * HEAD_DIM, D_OUT), ((0, 1024),), -0.2, 0.2)), 9.999999974752427e-07, 0.0001)
    gradient = scatter_about(key_list[6], (HEADS * HEAD_DIM, D_OUT), 0.03, 0.18, ((0, 1024),), jnp.float32)
    return dict(queries=queries, keys=keys, values=values, master=master, moment=moment, second=second, gradient=gradient)


beta_first = 0.9
beta_second = 0.999
learning_rate = 0.1
weight_decay = 0.1
epsilon = 1e-08
step_count = 10.0

def adamw(master, moment, second, gradient):
    moment_new = beta_first * moment + (1.0 - beta_first) * gradient
    second_new = beta_second * second + (1.0 - beta_second) * gradient * gradient
    moment_hat = moment_new / (1.0 - beta_first ** step_count)
    second_hat = second_new / (1.0 - beta_second ** step_count)
    return master - learning_rate * (moment_hat / (jnp.sqrt(second_hat) + epsilon) + weight_decay * master)

def attend_head(triple):
    query_rows, key_rows, value_rows = triple
    scores = jnp.dot(query_rows, key_rows.T, preferred_element_type=jnp.float32) * HEAD_DIM ** (-0.5)
    positions = jnp.arange(LENGTH)
    causal = positions[:, None] >= positions[None, :]
    scores = jnp.where(causal, scores, -jnp.inf)
    highest = lax.optimization_barrier(jnp.max(scores, axis=1, keepdims=True))
    expons = jnp.exp(scores - highest)
    denominator = lax.optimization_barrier(jnp.sum(expons, axis=1, keepdims=True))
    probs = (expons / denominator).astype(jnp.bfloat16)
    return jnp.dot(probs, value_rows, preferred_element_type=jnp.float32).astype(jnp.bfloat16)

def heads_first(array):
    return array.reshape(SEQS, LENGTH, HEADS, HEAD_DIM).transpose(0, 2, 1, 3).reshape(SEQS * HEADS, LENGTH, HEAD_DIM)

def reference(queries, keys, values, master, moment, second, gradient):
    attended = lax.map(attend_head, (heads_first(queries), heads_first(keys), heads_first(values)))
    attended = attended.reshape(SEQS, HEADS, LENGTH, HEAD_DIM).transpose(0, 2, 1, 3).reshape(SEQS * LENGTH, HEADS * HEAD_DIM)
    new_master = adamw(master, moment, second, gradient)
    weight = new_master.astype(jnp.bfloat16)
    projected = jnp.dot(attended, weight, preferred_element_type=jnp.float32).astype(jnp.bfloat16)
    return (projected.reshape(SEQS, LENGTH, D_OUT), new_master)
```

```python
import math

import jax
import jax.numpy as jnp
from jax import lax
from jax.experimental import pallas as pl
from jax.experimental.pallas import tpu as pltpu
from jax.sharding import Mesh
from jax.sharding import PartitionSpec as P

MESH = pl.DeviceIdType.MESH
AXES = ("x", "h", "c", "l", "z")
SIZES = (4, 2, 2, 4, 16)
HEAD_DIM = 128
SCALE = math.log2(math.e) / math.sqrt(HEAD_DIM)

beta_first = 0.9
beta_second = 0.999
learning_rate = 0.1
weight_decay = 0.1
epsilon = 1e-08
step_count = 10.0


def adamw(master, moment, second, gradient):
    moment_new = beta_first * moment + (1.0 - beta_first) * gradient
    second_new = beta_second * second + (1.0 - beta_second) * gradient * gradient
    moment_hat = moment_new / (1.0 - beta_first**step_count)
    second_hat = second_new / (1.0 - beta_second**step_count)
    return master - learning_rate * (
        moment_hat / (jnp.sqrt(second_hat) + epsilon) + weight_decay * master
    )


def kernel(
    q_in, k_in, v_in, ma, mo, se, gr,
    out, nm_out,
    qb, kb, vb, acc, mx, osrc, ob, oacc, wg, wsrc, wrecv, wasm,
    qs, qr, ks, kr, vs, vr, yks, ykr, yvs, yvr,
    w1s, w1r, w2s, w2r, w3s, w3r, zps, zpr, zms, zmr, sos, sor, sps, spr, sms, smr,
    os, orr,
):
    x, h, c, l, z = (lax.axis_index(a) for a in AXES)
    slot = x * 2 + c
    y = h * 4 + l
    z_hi = z // 8
    z_lo = z % 8

    def dev(**kw):
        d = {"x": x, "h": h, "c": c, "l": l, "z": z}
        d.update(kw)
        return d

    def half_peer(k):
        p = (slot + k) % 8
        return p, dev(x=p // 2, c=p % 2)

    def chip_peer(dx, dc):
        px, pc = (x + dx) % 4, (c + dc) % 2
        return px * 2 + pc, dev(x=px, c=pc)

    def y_peer(dy):
        p = (y + dy) % 8
        return p, dev(h=p // 4, l=p % 4)

    partner = dev(h=1 - h)
    sibling = dev(c=1 - c)
    z_next = dev(z=(z + 1) % 16)
    z_prev = dev(z=(z + 15) % 16)

    def remote(src, dst, ss, rs, to):
        return pltpu.make_async_remote_copy(
            src_ref=src, dst_ref=dst, send_sem=ss, recv_sem=rs, device_id=to, device_id_type=MESH
        )

    def landed(ref, sem):
        pltpu.make_async_copy(ref, ref, sem).wait()

    barrier = pltpu.get_barrier_semaphore()
    greeted = [y_peer(d)[1] for d in range(1, 8)]
    greeted += [dev(z=z_hi * 8 + (z_lo + d) % 8) for d in range(1, 8)]
    greeted += [half_peer(d)[1] for d in range(1, 8)]
    greeted += [z_next, z_prev]
    for to in greeted:
        pl.semaphore_signal(barrier, inc=1, device_id=to, device_id_type=MESH)

    new_master = adamw(ma[...], mo[...], se[...], gr[...])
    nm_out[...] = new_master
    for b in range(8):
        wsrc[b] = new_master[:, b * 128 : (b + 1) * 128]

    pl.semaphore_wait(barrier, len(greeted))

    sends = []

    def start(cp):
        cp.start()
        sends.append(cp)

    order = [(0, 1)] + [(dx, dc) for dc in (0, 1) for dx in (3, 1)] + [(2, 0), (2, 1)]

    def cols(p):
        return pl.ds(pl.multiple_of(p * 256, 256), 256)

    pltpu.make_async_copy(k_in.at[0, :, cols(slot)], kb.at[h, slot], kr.at[slot]).start()
    pltpu.make_async_copy(v_in.at[0, :, cols(slot)], vb.at[h, slot], vr.at[slot]).start()
    pltpu.make_async_copy(wsrc.at[z_lo], wrecv.at[z_lo], w1r.at[z_lo]).start()
    for d in range(1, 8):
        p = (z_lo + d) % 8
        start(remote(wsrc.at[p], wrecv.at[z_lo], w1s.at[d], w1r.at[z_lo], dev(z=z_hi * 8 + p)))
    for n, (dx, dc) in enumerate(order):
        p, to = chip_peer(dx, dc)
        start(remote(k_in.at[0, :, cols(p)], kb.at[h, slot], ks.at[n], kr.at[slot], to))
        start(remote(v_in.at[0, :, cols(p)], vb.at[h, slot], vs.at[n], vr.at[slot], to))

    def relay(t, j):
        landed(kb.at[h, j], kr.at[j])
        landed(vb.at[h, j], vr.at[j])

        @pl.when(jnp.logical_or(h == 0, j < 6))
        def _():
            remote(kb.at[h, j], kb.at[h, j], yks.at[t], ykr.at[j], partner).start()
            remote(vb.at[h, j], vb.at[h, j], yvs.at[t], yvr.at[j], partner).start()

    def relay_sent(t, j):
        @pl.when(jnp.logical_or(h == 0, j < 6))
        def _():
            remote(kb.at[h, j], kb.at[h, j], yks.at[t], ykr.at[j], partner).wait_send()
            remote(vb.at[h, j], vb.at[h, j], yvs.at[t], yvr.at[j], partner).wait_send()

    slots = [slot, x * 2 + (1 - c)]
    for t in range(3):
        g = jnp.where(t >= x, t + 1, t)
        slots += [2 * g, 2 * g + 1]

    relay(0, slots[0])
    relay(1, slots[1])

    for i in range(8):
        landed(wrecv.at[i], w1r.at[i])
    for i in range(8):
        wasm[2 * i : 2 * i + 2, :] = wrecv[i]
    wg[z, c, x, y] = wasm[...].astype(jnp.bfloat16)

    for d in range(1, 8):
        p, to = y_peer(d)
        start(remote(wg.at[z, c, x, y], wg.at[z, c, x, y], w2s.at[d], w2r.at[y], to))

    relay(2, slots[2])
    relay(3, slots[3])

    for d in range(1, 8):
        p = (y + d) % 8
        landed(wg.at[z, c, x, p], w2r.at[p])
    for d in range(1, 4):
        px = (x + d) % 4
        start(remote(wg.at[z, c, x], wg.at[z, c, x], w3s.at[d], w3r.at[x], dev(x=px)))

    pltpu.make_async_copy(q_in.at[0, :, cols(slot)], qb.at[slot], qr.at[slot]).start()
    for n, (dx, dc) in enumerate(order):
        p, to = chip_peer(dx, dc)
        start(remote(q_in.at[0, :, cols(p)], qb.at[slot], qs.at[n], qr.at[slot], to))

    for t in range(4, 8):
        relay(t, slots[t])

    for d in range(1, 4):
        px = (x + d) % 4
        landed(wg.at[z, c, px], w3r.at[px])

    def part(zc, u):
        return wg.at[zc, c, pl.ds(2 * u, 2)]

    def sib_part(zc, u):
        return wg.at[zc, 1 - c, pl.ds(2 * u, 2)]

    for u in range(2):
        start(remote(part(z, u), part(z, u), zps.at[0, u], zpr.at[0, u], z_next))
        start(remote(part(z, u), part(z, u), zms.at[0, u], zmr.at[0, u], z_prev))
    for u in range(2):
        start(remote(part(z, u), part(z, u), sos.at[u], sor.at[u], sibling))

    def ring(t):
        zp = (z + 15 - t) % 16
        zm = (z + 1 + t) % 16
        for u in range(2):
            landed(part(zp, u), zpr.at[t, u])
            if t < 7:
                start(remote(part(zp, u), part(zp, u), zps.at[t + 1, u], zpr.at[t + 1, u], z_next))
            if t < 7:
                landed(part(zm, u), zmr.at[t, u])
                if t < 6:
                    start(remote(part(zm, u), part(zm, u), zms.at[t + 1, u], zmr.at[t + 1, u], z_prev))
                start(remote(part(zm, u), part(zm, u), sms.at[t, u], smr.at[t, u], sibling))
            start(remote(part(zp, u), part(zp, u), sps.at[t, u], spr.at[t, u], sibling))

    def attend(qg, kh, kg, diagonal):
        for hh in range(2):
            lanes = slice(hh * 128, hh * 128 + 128)
            q = qb[pl.ds(2 * qg, 2), :, lanes].reshape(256, 128)
            k = kb[kh, pl.ds(2 * kg, 2), :, lanes].reshape(256, 128)
            v = vb[kh, pl.ds(2 * kg, 2), :, lanes].reshape(256, 128)
            s = lax.dot_general(q, k, (((1,), (1,)), ((), ())), preferred_element_type=jnp.float32)
            s = s * SCALE
            if diagonal:
                rows = lax.broadcasted_iota(jnp.int32, (256, 256), 0)
                keys = lax.broadcasted_iota(jnp.int32, (256, 256), 1)
                s = jnp.where(rows >= keys, s, -jnp.inf)
            top = jnp.broadcast_to(jnp.max(s, axis=1, keepdims=True), (256, 128))
            v1 = jnp.concatenate([v, jnp.ones((256, 128), jnp.bfloat16)], axis=1)
            if diagonal:
                new = top
            else:
                old = mx[hh, qg]
                new = jnp.maximum(old, top)
            p = jnp.exp2(s - jnp.concatenate([new, new], axis=1)).astype(jnp.bfloat16)
            pv = jnp.dot(p, v1, preferred_element_type=jnp.float32)
            if diagonal:
                acc[hh, qg] = pv
            else:
                fade = jnp.exp2(old - new)
                acc[hh, qg] = acc[hh, qg] * jnp.concatenate([fade, fade], axis=1) + pv
            mx[hh, qg] = new

    def own(qg):
        attend(qg, h, qg, True)

        def step(g, _):
            attend(qg, h, g, False)
            return 0

        lax.fori_loop(0, qg, step, 0)

    def give(d):
        for hh in range(2):
            total = acc[hh, d]
            o = (total[:, :128] / total[:, 128:]).astype(jnp.bfloat16)
            for cc in range(2):
                osrc[d, cc, :, hh * 128 : hh * 128 + 128] = o[cc * 128 : cc * 128 + 128]
        for cc in range(2):
            self_ = jnp.logical_and(d == x, cc == c)

            @pl.when(self_)
            def _():
                pltpu.make_async_copy(osrc.at[d, cc], ob.at[slot], orr.at[slot]).start()

            @pl.when(jnp.logical_not(self_))
            def _():
                remote(osrc.at[d, cc], ob.at[slot], os.at[d, cc], orr.at[slot], dev(x=d, c=cc)).start()

    def given(d):
        for cc in range(2):
            @pl.when(jnp.logical_not(jnp.logical_and(d == x, cc == c)))
            def _():
                remote(osrc.at[d, cc], ob.at[slot], os.at[d, cc], orr.at[slot], dev(x=d, c=cc)).wait_send()

    def cross(g):
        for j in (2 * g, 2 * g + 1):
            landed(kb.at[1 - h, j], ykr.at[j])
            landed(vb.at[1 - h, j], yvr.at[j])

        def step(qg, _):
            attend(qg, 1 - h, g, False)
            return 0

        lax.fori_loop(g + 1 - h, 4, step, 0)

    for j in range(8):
        landed(qb.at[j], qr.at[j])
    own(0)

    @pl.when(h == 0)
    def _():
        give(0)

    own(1)
    ring(0)
    own(2)
    ring(1)
    own(3)
    ring(2)
    cross(0)
    give(1 - h)
    ring(3)
    cross(1)
    give(2 - h)
    ring(4)
    ring(5)
    ring(6)
    cross(2)
    give(3 - h)
    ring(7)

    @pl.when(h == 1)
    def _():
        cross(3)
        give(3)

    for u in range(2):
        landed(sib_part(z, u), sor.at[u])
        for t in range(8):
            landed(sib_part((z + 15 - t) % 16, u), spr.at[t, u])
        for t in range(7):
            landed(sib_part((z + 1 + t) % 16, u), smr.at[t, u])

    def project(j, first):
        landed(ob.at[j], orr.at[j])
        o = ob[j]
        wx, wh = j // 2, j % 2
        for nb in range(4):
            rhs = jnp.concatenate(
                [
                    jnp.concatenate(
                        [
                            wg[zh * 8 + b, cc, wx, wh * 4 + ll]
                            for cc in range(2)
                            for ll in range(4)
                            for zh in range(2)
                        ],
                        axis=0,
                    )
                    for b in (2 * nb, 2 * nb + 1)
                ],
                axis=1,
            )
            r = jnp.dot(o, rhs, preferred_element_type=jnp.float32)
            at = slice(nb * 256, nb * 256 + 256)
            oacc[:, at] = r if first else oacc[:, at] + r

    project(0, True)

    def more(j, _):
        project(j, False)
        return 0

    lax.fori_loop(1, 8, more, 0)
    out[...] = oacc[...].astype(jnp.bfloat16)

    for cp in sends:
        cp.wait_send()
    for t in range(8):
        relay_sent(t, slots[t])
    for d in range(4):
        given(d)


def body(queries, keys, values, master, moment, second, gradient):
    bf, f32 = jnp.bfloat16, jnp.float32
    dma = pltpu.SemaphoreType.DMA
    any_ = pl.BlockSpec(memory_space=pl.ANY)
    vmem = pl.BlockSpec(memory_space=pltpu.VMEM)
    projected, new_master = pl.pallas_call(
        kernel,
        name="attn_step",
        out_shape=(
            jax.ShapeDtypeStruct((128, 1024), bf),
            jax.ShapeDtypeStruct((2, 1024), f32),
        ),
        in_specs=[any_] * 3 + [vmem] * 4,
        out_specs=(vmem, vmem),
        scratch_shapes=[
            pltpu.VMEM((8, 128, 256), bf),
            pltpu.VMEM((2, 8, 128, 256), bf),
            pltpu.VMEM((2, 8, 128, 256), bf),
            pltpu.VMEM((2, 4, 256, 256), f32),
            pltpu.VMEM((2, 4, 256, 128), f32),
            pltpu.VMEM((4, 2, 128, 256), bf),
            pltpu.VMEM((8, 128, 256), bf),
            pltpu.VMEM((128, 1024), f32),
            pltpu.VMEM((16, 2, 4, 8, 16, 128), bf),
            pltpu.VMEM((8, 2, 128), f32),
            pltpu.VMEM((8, 2, 128), f32),
            pltpu.VMEM((16, 128), f32),
            dma((7,)), dma((8,)), dma((7,)), dma((8,)), dma((7,)), dma((8,)),
            dma((8,)), dma((8,)), dma((8,)), dma((8,)),
            dma((8,)), dma((8,)), dma((8,)), dma((8,)), dma((4,)), dma((4,)),
            dma((8, 2)), dma((8, 2)), dma((7, 2)), dma((7, 2)),
            dma((2,)), dma((2,)), dma((8, 2)), dma((8, 2)), dma((7, 2)), dma((7, 2)),
            dma((4, 2)), dma((8,)),
        ],
        compiler_params=pltpu.CompilerParams(collective_id=1, has_side_effects=True),
    )(queries, keys, values, master, moment, second, gradient)
    return projected[None], new_master


def solution(mesh):
    torus = Mesh(mesh.devices.reshape(SIZES), AXES)
    tokens = P(("l", "z"), ("x", "h", "c"), None)
    rows = P(AXES, None)
    return jax.shard_map(
        body,
        mesh=torus,
        in_specs=(tokens,) * 3 + (rows,) * 4,
        out_specs=(tokens, rows),
        check_vma=False,
    )
```

```python
import math

import jax
import jax.numpy as jnp
from jax import lax
from jax.experimental import pallas as pl
from jax.experimental.pallas import tpu as pltpu
from jax.sharding import Mesh
from jax.sharding import PartitionSpec as P

MESH = pl.DeviceIdType.MESH
AXES = ("x", "h", "c", "l", "z")
SIZES = (4, 2, 2, 4, 16)
HEAD_DIM = 128
SCALE = math.log2(math.e) / math.sqrt(HEAD_DIM)

beta_first = 0.9
beta_second = 0.999
learning_rate = 0.1
weight_decay = 0.1
epsilon = 1e-08
step_count = 10.0


def adamw(master, moment, second, gradient):
    moment_new = beta_first * moment + (1.0 - beta_first) * gradient
    second_new = beta_second * second + (1.0 - beta_second) * gradient * gradient
    moment_hat = moment_new / (1.0 - beta_first**step_count)
    second_hat = second_new / (1.0 - beta_second**step_count)
    return master - learning_rate * (
        moment_hat / (jnp.sqrt(second_hat) + epsilon) + weight_decay * master
    )


def kernel(
    q_in, k_in, v_in, ma, mo, se, gr,
    out, nm_out,
    qb, kb, vb, acc, mx, osrc, ob, oacc, wg, wf, wasm,
    qs, qr, ks, kr, vs, vr, yks, ykr, yvs, yvr,
    w2s, w2r, w3s, w3r, zps, zpr, zms, zmr, sos, sor, sps, spr, sms, smr,
    os, orr,
):
    x, h, c, l, z = (lax.axis_index(a) for a in AXES)
    slot = x * 2 + c
    y = h * 4 + l
    odd = z % 2

    def dev(**kw):
        d = {"x": x, "h": h, "c": c, "l": l, "z": z}
        d.update(kw)
        return d

    def half_peer(k):
        p = (slot + k) % 8
        return p, dev(x=p // 2, c=p % 2)

    def chip_peer(dx, dc):
        px, pc = (x + dx) % 4, (c + dc) % 2
        return px * 2 + pc, dev(x=px, c=pc)

    def y_peer(dy):
        p = (y + dy) % 8
        return p, dev(h=p // 4, l=p % 4)

    partner = dev(h=1 - h)
    sibling = dev(c=1 - c)
    z_next = dev(z=(z + 1) % 16)
    z_prev = dev(z=(z + 15) % 16)

    def remote(src, dst, ss, rs, to):
        return pltpu.make_async_remote_copy(
            src_ref=src, dst_ref=dst, send_sem=ss, recv_sem=rs, device_id=to, device_id_type=MESH
        )

    def landed(ref, sem):
        pltpu.make_async_copy(ref, ref, sem).wait()

    barrier = pltpu.get_barrier_semaphore()
    greeted = [y_peer(d)[1] for d in range(1, 8)]
    greeted += [half_peer(d)[1] for d in range(1, 8)]
    for to in greeted:
        pl.semaphore_signal(barrier, inc=1, device_id=to, device_id_type=MESH)

    new_master = adamw(ma[...], mo[...], se[...], gr[...])
    nm_out[...] = new_master
    for r in range(2):
        for b in range(8):
            wasm[8 * r + b : 8 * r + b + 1, :] = new_master[r : r + 1, b * 128 : (b + 1) * 128]
    wg[z, c, x, y] = wasm[...].astype(jnp.bfloat16)

    pl.semaphore_wait(barrier, len(greeted) + 2 * odd)
    for to in (z_next, z_prev):
        pl.semaphore_signal(barrier, inc=1, device_id=to, device_id_type=MESH)

    sends = []

    def start(cp):
        cp.start()
        sends.append(cp)

    order = [(0, 1)] + [(dx, dc) for dc in (0, 1) for dx in (3, 1)] + [(2, 0), (2, 1)]

    def cols(p):
        return pl.ds(pl.multiple_of(p * 256, 256), 256)

    pltpu.make_async_copy(k_in.at[0, :, cols(slot)], kb.at[h, slot], kr.at[slot]).start()
    pltpu.make_async_copy(v_in.at[0, :, cols(slot)], vb.at[h, slot], vr.at[slot]).start()
    for d in range(1, 8):
        p, to = y_peer(d)
        start(remote(wg.at[z, c, x, y], wg.at[z, c, x, y], w2s.at[d], w2r.at[y], to))
    for n, (dx, dc) in enumerate(order):
        p, to = chip_peer(dx, dc)
        start(remote(k_in.at[0, :, cols(p)], kb.at[h, slot], ks.at[n], kr.at[slot], to))
        start(remote(v_in.at[0, :, cols(p)], vb.at[h, slot], vs.at[n], vr.at[slot], to))

    def relay(t, j):
        landed(kb.at[h, j], kr.at[j])
        landed(vb.at[h, j], vr.at[j])

        @pl.when(jnp.logical_or(h == 0, j < 6))
        def _():
            remote(kb.at[h, j], kb.at[h, j], yks.at[t], ykr.at[j], partner).start()
            remote(vb.at[h, j], vb.at[h, j], yvs.at[t], yvr.at[j], partner).start()

    def relay_sent(t, j):
        @pl.when(jnp.logical_or(h == 0, j < 6))
        def _():
            remote(kb.at[h, j], kb.at[h, j], yks.at[t], ykr.at[j], partner).wait_send()
            remote(vb.at[h, j], vb.at[h, j], yvs.at[t], yvr.at[j], partner).wait_send()

    slots = [slot, x * 2 + (1 - c)]
    for t in range(3):
        g = jnp.where(t >= x, t + 1, t)
        slots += [2 * g, 2 * g + 1]

    relay(0, slots[0])
    relay(1, slots[1])

    for d in range(1, 8):
        p = (y + d) % 8
        landed(wg.at[z, c, x, p], w2r.at[p])
    for d in range(1, 4):
        px = (x + d) % 4
        start(remote(wg.at[z, c, x], wg.at[z, c, x], w3s.at[d], w3r.at[x], dev(x=px)))

    pltpu.make_async_copy(q_in.at[0, :, cols(slot)], qb.at[slot], qr.at[slot]).start()
    for n, (dx, dc) in enumerate(order):
        p, to = chip_peer(dx, dc)
        start(remote(q_in.at[0, :, cols(p)], qb.at[slot], qs.at[n], qr.at[slot], to))

    for t in range(2, 8):
        relay(t, slots[t])

    for d in range(1, 4):
        px = (x + d) % 4
        landed(wg.at[z, c, px], w3r.at[px])

    def part(zc, u):
        return wg.at[zc, c, pl.ds(2 * u, 2)]

    def sib_part(zc, u):
        return wg.at[zc, 1 - c, pl.ds(2 * u, 2)]

    @pl.when(odd == 0)
    def _():
        pl.semaphore_wait(barrier, 2)

    for u in range(2):
        start(remote(part(z, u), part(z, u), zps.at[0, u], zpr.at[0, u], z_next))
        start(remote(part(z, u), part(z, u), zms.at[0, u], zmr.at[0, u], z_prev))
    for u in range(2):
        start(remote(part(z, u), part(z, u), sos.at[u], sor.at[u], sibling))

    def scatter(zc, cc):
        def some(i, _):
            xi, hi = i // 2, i % 2
            base = (xi * 4 + hi * 2 + cc) * 128 + 2 * zc
            for ll in range(4):
                t = wg[zc, cc, xi, hi * 4 + ll].astype(jnp.float32)
                for r in range(2):
                    wf[pl.ds(base + 32 * ll + r, 8, stride=2048), :] = t[8 * r : 8 * r + 8]
            return 0

        lax.fori_loop(0, 8, some, 0)

    def sibling_planes(t):
        zp = (z + 15 - t) % 16
        zm = (z + 1 + t) % 16
        for u in range(2):
            landed(sib_part(zp, u), spr.at[t, u])
            if t < 7:
                landed(sib_part(zm, u), smr.at[t, u])
        scatter(zp, 1 - c)
        if t < 7:
            scatter(zm, 1 - c)

    def ring(t):
        zp = (z + 15 - t) % 16
        zm = (z + 1 + t) % 16
        for u in range(2):
            landed(part(zp, u), zpr.at[t, u])
            if t < 7:
                start(remote(part(zp, u), part(zp, u), zps.at[t + 1, u], zpr.at[t + 1, u], z_next))
            if t < 7:
                landed(part(zm, u), zmr.at[t, u])
                if t < 6:
                    start(remote(part(zm, u), part(zm, u), zms.at[t + 1, u], zmr.at[t + 1, u], z_prev))
                start(remote(part(zm, u), part(zm, u), sms.at[t, u], smr.at[t, u], sibling))
            start(remote(part(zp, u), part(zp, u), sps.at[t, u], spr.at[t, u], sibling))
        scatter(zp, c)
        if t < 7:
            scatter(zm, c)
        if t > 0:
            sibling_planes(t - 1)
        else:
            scatter(z, c)
            for u in range(2):
                landed(sib_part(z, u), sor.at[u])
            scatter(z, 1 - c)

    def attend(qg, kh, kg, diagonal):
        for hh in range(2):
            lanes = slice(hh * 128, hh * 128 + 128)
            q = qb[pl.ds(2 * qg, 2), :, lanes].reshape(256, 128)
            k = kb[kh, pl.ds(2 * kg, 2), :, lanes].reshape(256, 128)
            v = vb[kh, pl.ds(2 * kg, 2), :, lanes].reshape(256, 128)
            s = lax.dot_general(q, k, (((1,), (1,)), ((), ())), preferred_element_type=jnp.float32)
            s = s * SCALE
            if diagonal:
                rows = lax.broadcasted_iota(jnp.int32, (256, 256), 0)
                keys = lax.broadcasted_iota(jnp.int32, (256, 256), 1)
                s = jnp.where(rows >= keys, s, -jnp.inf)
            top = jnp.broadcast_to(jnp.max(s, axis=1, keepdims=True), (256, 128))
            v1 = jnp.concatenate([v, jnp.ones((256, 128), jnp.bfloat16)], axis=1)
            if diagonal:
                new = top
            else:
                old = mx[hh, qg]
                new = jnp.maximum(old, top)
            p = jnp.exp2(s - jnp.concatenate([new, new], axis=1)).astype(jnp.bfloat16)
            pv = jnp.dot(p, v1, preferred_element_type=jnp.float32)
            if diagonal:
                acc[hh, qg] = pv
            else:
                fade = jnp.exp2(old - new)
                acc[hh, qg] = acc[hh, qg] * jnp.concatenate([fade, fade], axis=1) + pv
            mx[hh, qg] = new

    def own(qg):
        attend(qg, h, qg, True)

        def step(g, _):
            attend(qg, h, g, False)
            return 0

        lax.fori_loop(0, qg, step, 0)

    def give(d):
        for hh in range(2):
            total = acc[hh, d]
            o = (total[:, :128] / total[:, 128:]).astype(jnp.bfloat16)
            for cc in range(2):
                osrc[d, cc, :, hh * 128 : hh * 128 + 128] = o[cc * 128 : cc * 128 + 128]
        for cc in range(2):
            self_ = jnp.logical_and(d == x, cc == c)

            @pl.when(self_)
            def _():
                pltpu.make_async_copy(osrc.at[d, cc], ob.at[slot], orr.at[slot]).start()

            @pl.when(jnp.logical_not(self_))
            def _():
                remote(osrc.at[d, cc], ob.at[slot], os.at[d, cc], orr.at[slot], dev(x=d, c=cc)).start()

    def given(d):
        for cc in range(2):
            @pl.when(jnp.logical_not(jnp.logical_and(d == x, cc == c)))
            def _():
                remote(osrc.at[d, cc], ob.at[slot], os.at[d, cc], orr.at[slot], dev(x=d, c=cc)).wait_send()

    def cross(g):
        for j in (2 * g, 2 * g + 1):
            landed(kb.at[1 - h, j], ykr.at[j])
            landed(vb.at[1 - h, j], yvr.at[j])

        def step(qg, _):
            attend(qg, 1 - h, g, False)
            return 0

        lax.fori_loop(g + 1 - h, 4, step, 0)

    for j in range(8):
        landed(qb.at[j], qr.at[j])
    own(0)

    @pl.when(h == 0)
    def _():
        give(0)

    own(1)
    ring(0)
    own(2)
    ring(1)
    own(3)
    cross(0)
    give(1 - h)
    ring(2)
    ring(3)
    cross(1)
    give(2 - h)
    ring(4)
    ring(5)
    cross(2)
    give(3 - h)
    ring(6)

    @pl.when(h == 1)
    def _():
        cross(3)
        give(3)

    ring(7)
    sibling_planes(7)

    def project(j, first):
        landed(ob.at[j], orr.at[j])
        o = ob[j]
        for nb in range(4):
            rhs = jnp.concatenate(
                [
                    wf[pl.ds(pl.multiple_of(b * 2048 + 256 * j, 256), 256), :].astype(jnp.bfloat16)
                    for b in (2 * nb, 2 * nb + 1)
                ],
                axis=1,
            )
            r = jnp.dot(o, rhs, preferred_element_type=jnp.float32)
            at = slice(nb * 256, nb * 256 + 256)
            oacc[:, at] = r if first else oacc[:, at] + r

    project(0, True)

    def more(j, _):
        project(j, False)
        return 0

    lax.fori_loop(1, 8, more, 0)
    out[...] = oacc[...].astype(jnp.bfloat16)

    for cp in sends:
        cp.wait_send()
    for t in range(8):
        relay_sent(t, slots[t])
    for d in range(4):
        given(d)


def body(queries, keys, values, master, moment, second, gradient):
    bf, f32 = jnp.bfloat16, jnp.float32
    dma = pltpu.SemaphoreType.DMA
    any_ = pl.BlockSpec(memory_space=pl.ANY)
    vmem = pl.BlockSpec(memory_space=pltpu.VMEM)
    projected, new_master = pl.pallas_call(
        kernel,
        name="attn_step",
        out_shape=(
            jax.ShapeDtypeStruct((128, 1024), bf),
            jax.ShapeDtypeStruct((2, 1024), f32),
        ),
        in_specs=[any_] * 3 + [vmem] * 4,
        out_specs=(vmem, vmem),
        scratch_shapes=[
            pltpu.VMEM((8, 128, 256), bf),
            pltpu.VMEM((2, 8, 128, 256), bf),
            pltpu.VMEM((2, 8, 128, 256), bf),
            pltpu.VMEM((2, 4, 256, 256), f32),
            pltpu.VMEM((2, 4, 256, 128), f32),
            pltpu.VMEM((4, 2, 128, 256), bf),
            pltpu.VMEM((8, 128, 256), bf),
            pltpu.VMEM((128, 1024), f32),
            pltpu.VMEM((16, 2, 4, 8, 16, 128), bf),
            pltpu.VMEM((8 * 2048, 128), f32),
            pltpu.VMEM((16, 128), f32),
            dma((7,)), dma((8,)), dma((7,)), dma((8,)), dma((7,)), dma((8,)),
            dma((8,)), dma((8,)), dma((8,)), dma((8,)),
            dma((8,)), dma((8,)), dma((4,)), dma((4,)),
            dma((8, 2)), dma((8, 2)), dma((7, 2)), dma((7, 2)),
            dma((2,)), dma((2,)), dma((8, 2)), dma((8, 2)), dma((7, 2)), dma((7, 2)),
            dma((4, 2)), dma((8,)),
        ],
        compiler_params=pltpu.CompilerParams(collective_id=1, has_side_effects=True),
    )(queries, keys, values, master, moment, second, gradient)
    return projected[None], new_master


def solution(mesh):
    torus = Mesh(mesh.devices.reshape(SIZES), AXES)
    tokens = P(("l", "z"), ("x", "h", "c"), None)
    rows = P(AXES, None)
    return jax.shard_map(
        body,
        mesh=torus,
        in_specs=(tokens,) * 3 + (rows,) * 4,
        out_specs=(tokens, rows),
        check_vma=False,
    )
```

```python
import math

import jax
import jax.numpy as jnp
from jax import lax
from jax.experimental import pallas as pl
from jax.experimental.pallas import tpu as pltpu
from jax.sharding import Mesh
from jax.sharding import PartitionSpec as P

MESH = pl.DeviceIdType.MESH
AXES = ("x", "h", "c", "l", "z")
SIZES = (4, 2, 2, 4, 16)
HEAD_DIM = 128
SCALE = math.log2(math.e) / math.sqrt(HEAD_DIM)

beta_first = 0.9
beta_second = 0.999
learning_rate = 0.1
weight_decay = 0.1
epsilon = 1e-08
step_count = 10.0


def adamw(master, moment, second, gradient):
    moment_new = beta_first * moment + (1.0 - beta_first) * gradient
    second_new = beta_second * second + (1.0 - beta_second) * gradient * gradient
    moment_hat = moment_new / (1.0 - beta_first**step_count)
    second_hat = second_new / (1.0 - beta_second**step_count)
    return master - learning_rate * (
        moment_hat / (jnp.sqrt(second_hat) + epsilon) + weight_decay * master
    )


def kernel(
    q_in, k_in, v_in, ma, mo, se, gr,
    out, nm_out,
    qb, kb, vb, acc, mx, osrc, ob, oacc, wg, wsrc, wrecv, wasm, perm,
    qs, qr, ks, kr, vs, vr, yks, ykr, yvs, yvr,
    w1s, w1r, w2s, w2r, w3s, w3r, zps, zpr, zms, zmr, sos, sor, sps, spr, sms, smr,
    os, orr,
):
    x, h, c, l, z = (lax.axis_index(a) for a in AXES)
    slot = x * 2 + c
    y = h * 4 + l
    odd = z % 2

    def dev(**kw):
        d = {"x": x, "h": h, "c": c, "l": l, "z": z}
        d.update(kw)
        return d

    def half_peer(k):
        p = (slot + k) % 8
        return p, dev(x=p // 2, c=p % 2)

    def chip_peer(dx, dc):
        px, pc = (x + dx) % 4, (c + dc) % 2
        return px * 2 + pc, dev(x=px, c=pc)

    def y_peer(dy):
        p = (y + dy) % 8
        return p, dev(h=p // 4, l=p % 4)

    partner = dev(h=1 - h)
    sibling = dev(c=1 - c)
    z_next = dev(z=(z + 1) % 16)
    z_prev = dev(z=(z + 15) % 16)

    def remote(src, dst, ss, rs, to):
        return pltpu.make_async_remote_copy(
            src_ref=src, dst_ref=dst, send_sem=ss, recv_sem=rs, device_id=to, device_id_type=MESH
        )

    def landed(ref, sem):
        pltpu.make_async_copy(ref, ref, sem).wait()

    barrier = pltpu.get_barrier_semaphore()
    greeted = [y_peer(d)[1] for d in range(1, 8)]
    greeted += [half_peer(d)[1] for d in range(1, 8)]
    for to in greeted:
        pl.semaphore_signal(barrier, inc=1, device_id=to, device_id_type=MESH)

    new_master = adamw(ma[...], mo[...], se[...], gr[...])
    nm_out[...] = new_master
    for b in range(8):
        wsrc[b] = new_master[:, b * 128 : (b + 1) * 128]

    pl.semaphore_wait(barrier, len(greeted) + 2 * odd)
    for to in (z_next, z_prev):
        pl.semaphore_signal(barrier, inc=1, device_id=to, device_id_type=MESH)

    sends = []

    def start(cp):
        cp.start()
        sends.append(cp)

    order = [(0, 1)] + [(dx, dc) for dc in (0, 1) for dx in (3, 1)] + [(2, 0), (2, 1)]

    def cols(p):
        return pl.ds(pl.multiple_of(p * 256, 256), 256)

    pltpu.make_async_copy(k_in.at[0, :, cols(slot)], kb.at[h, slot], kr.at[slot]).start()
    pltpu.make_async_copy(v_in.at[0, :, cols(slot)], vb.at[h, slot], vr.at[slot]).start()
    pltpu.make_async_copy(wsrc.at[y], wrecv.at[y], w1r.at[y]).start()
    for d in range(1, 8):
        p, to = y_peer(d)
        start(remote(wsrc.at[p], wrecv.at[y], w1s.at[d], w1r.at[y], to))
    for n, (dx, dc) in enumerate(order):
        p, to = chip_peer(dx, dc)
        start(remote(k_in.at[0, :, cols(p)], kb.at[h, slot], ks.at[n], kr.at[slot], to))
        start(remote(v_in.at[0, :, cols(p)], vb.at[h, slot], vs.at[n], vr.at[slot], to))

    def relay(t, j):
        landed(kb.at[h, j], kr.at[j])
        landed(vb.at[h, j], vr.at[j])

        @pl.when(jnp.logical_or(h == 0, j < 6))
        def _():
            remote(kb.at[h, j], kb.at[h, j], yks.at[t], ykr.at[j], partner).start()
            remote(vb.at[h, j], vb.at[h, j], yvs.at[t], yvr.at[j], partner).start()

    def relay_sent(t, j):
        @pl.when(jnp.logical_or(h == 0, j < 6))
        def _():
            remote(kb.at[h, j], kb.at[h, j], yks.at[t], ykr.at[j], partner).wait_send()
            remote(vb.at[h, j], vb.at[h, j], yvs.at[t], yvr.at[j], partner).wait_send()

    slots = [slot, x * 2 + (1 - c)]
    for t in range(3):
        g = jnp.where(t >= x, t + 1, t)
        slots += [2 * g, 2 * g + 1]

    relay(0, slots[0])
    relay(1, slots[1])

    for i in range(8):
        landed(wrecv.at[i], w1r.at[i])
    for i in range(8):
        wasm[2 * i : 2 * i + 2, :] = wrecv[i]
    wg[z, c, x, y] = wasm[...].astype(jnp.bfloat16)

    for d in range(1, 8):
        p, to = y_peer(d)
        start(remote(wg.at[z, c, x, y], wg.at[z, c, x, y], w2s.at[d], w2r.at[y], to))

    to_col = lax.broadcasted_iota(jnp.int32, (256, 256), 1)
    from_row = lax.broadcasted_iota(jnp.int32, (256, 256), 0)
    wanted = (
        ((to_col >> 3) & 1) * 128 + ((to_col >> 1) & 3) * 32 + (to_col >> 4) * 2 + (to_col & 1)
    )
    perm[...] = jnp.where(from_row == wanted, 1.0, 0.0).astype(jnp.bfloat16)

    for d in range(1, 8):
        p = (y + d) % 8
        landed(wg.at[z, c, x, p], w2r.at[p])
    for d in range(1, 4):
        px = (x + d) % 4
        start(remote(wg.at[z, c, x], wg.at[z, c, x], w3s.at[d], w3r.at[x], dev(x=px)))

    pltpu.make_async_copy(q_in.at[0, :, cols(slot)], qb.at[slot], qr.at[slot]).start()
    for n, (dx, dc) in enumerate(order):
        p, to = chip_peer(dx, dc)
        start(remote(q_in.at[0, :, cols(p)], qb.at[slot], qs.at[n], qr.at[slot], to))

    for t in range(2, 8):
        relay(t, slots[t])

    for d in range(1, 4):
        px = (x + d) % 4
        landed(wg.at[z, c, px], w3r.at[px])

    def part(zc, u):
        return wg.at[zc, c, u]

    @pl.when(odd == 0)
    def _():
        pl.semaphore_wait(barrier, 2)

    for u in range(4):
        start(remote(part(z, u), part(z, u), zps.at[0, u], zpr.at[0, u], z_next))
        start(remote(part(z, u), part(z, u), zms.at[0, u], zmr.at[0, u], z_prev))
    start(remote(wg.at[z, c], wg.at[z, c], sos.at[0], sor.at[0], sibling))

    def ring(t):
        zp = (z + 15 - t) % 16
        zm = (z + 1 + t) % 16
        for u in range(4):
            landed(part(zp, u), zpr.at[t, u])
            if t < 7:
                start(remote(part(zp, u), part(zp, u), zps.at[t + 1, u], zpr.at[t + 1, u], z_next))
                landed(part(zm, u), zmr.at[t, u])
            if t < 6:
                start(remote(part(zm, u), part(zm, u), zms.at[t + 1, u], zmr.at[t + 1, u], z_prev))
        start(remote(wg.at[zp, c], wg.at[zp, c], sps.at[t], spr.at[t], sibling))
        if t < 7:
            start(remote(wg.at[zm, c], wg.at[zm, c], sms.at[t], smr.at[t], sibling))

    def attend(qg, kh, kg, diagonal):
        for hh in range(2):
            lanes = slice(hh * 128, hh * 128 + 128)
            q = qb[pl.ds(2 * qg, 2), :, lanes].reshape(256, 128)
            k = kb[kh, pl.ds(2 * kg, 2), :, lanes].reshape(256, 128)
            v = vb[kh, pl.ds(2 * kg, 2), :, lanes].reshape(256, 128)
            s = lax.dot_general(q, k, (((1,), (1,)), ((), ())), preferred_element_type=jnp.float32)
            s = s * SCALE
            if diagonal:
                rows = lax.broadcasted_iota(jnp.int32, (256, 256), 0)
                keys = lax.broadcasted_iota(jnp.int32, (256, 256), 1)
                s = jnp.where(rows >= keys, s, -jnp.inf)
            top = jnp.broadcast_to(jnp.max(s, axis=1, keepdims=True), (256, 128))
            v1 = jnp.concatenate([v, jnp.ones((256, 128), jnp.bfloat16)], axis=1)
            if diagonal:
                new = top
            else:
                old = mx[hh, qg]
                new = jnp.maximum(old, top)
            p = jnp.exp2(s - jnp.concatenate([new, new], axis=1)).astype(jnp.bfloat16)
            pv = jnp.dot(p, v1, preferred_element_type=jnp.float32)
            if diagonal:
                acc[hh, qg] = pv
            else:
                fade = jnp.exp2(old - new)
                acc[hh, qg] = acc[hh, qg] * jnp.concatenate([fade, fade], axis=1) + pv
            mx[hh, qg] = new

    def own(qg):
        attend(qg, h, qg, True)

        def step(g, _):
            attend(qg, h, g, False)
            return 0

        lax.fori_loop(0, qg, step, 0)

    def give(d):
        for hh in range(2):
            total = acc[hh, d]
            o = (total[:, :128] / total[:, 128:]).astype(jnp.bfloat16)
            for cc in range(2):
                osrc[d, cc, :, hh * 128 : hh * 128 + 128] = o[cc * 128 : cc * 128 + 128]
        for cc in range(2):
            self_ = jnp.logical_and(d == x, cc == c)

            @pl.when(self_)
            def _():
                pltpu.make_async_copy(osrc.at[d, cc], ob.at[slot], orr.at[slot]).start()

            @pl.when(jnp.logical_not(self_))
            def _():
                remote(osrc.at[d, cc], ob.at[slot], os.at[d, cc], orr.at[slot], dev(x=d, c=cc)).start()

    def given(d):
        for cc in range(2):
            @pl.when(jnp.logical_not(jnp.logical_and(d == x, cc == c)))
            def _():
                remote(osrc.at[d, cc], ob.at[slot], os.at[d, cc], orr.at[slot], dev(x=d, c=cc)).wait_send()

    def cross(g):
        for j in (2 * g, 2 * g + 1):
            landed(kb.at[1 - h, j], ykr.at[j])
            landed(vb.at[1 - h, j], yvr.at[j])

        def step(qg, _):
            attend(qg, 1 - h, g, False)
            return 0

        lax.fori_loop(g + 1 - h, 4, step, 0)

    for j in range(8):
        landed(qb.at[j], qr.at[j])
    own(0)

    @pl.when(h == 0)
    def _():
        give(0)

    own(1)
    ring(0)
    own(2)
    ring(1)
    own(3)
    cross(0)
    give(1 - h)
    ring(2)
    cross(1)
    give(2 - h)
    ring(3)
    ring(4)
    ring(5)
    cross(2)
    give(3 - h)

    @pl.when(jnp.logical_and(h == 1, z < 8))
    def _():
        cross(3)
        give(3)

    ring(6)
    ring(7)

    @pl.when(jnp.logical_and(h == 1, z >= 8))
    def _():
        cross(3)
        give(3)

    landed(wg.at[z, 1 - c], sor.at[0])
    for t in range(8):
        landed(wg.at[(z + 15 - t) % 16, 1 - c], spr.at[t])
    for t in range(7):
        landed(wg.at[(z + 1 + t) % 16, 1 - c], smr.at[t])

    oacc[...] = jnp.zeros((128, 1024), jnp.float32)

    def project(i, _):
        landed(ob.at[2 * i], orr.at[2 * i])
        landed(ob.at[2 * i + 1], orr.at[2 * i + 1])
        for cc in range(2):
            lanes = slice(cc * 128, cc * 128 + 128)
            o = jnp.concatenate([ob[2 * i, :, lanes], ob[2 * i + 1, :, lanes]], axis=1)
            o = jnp.dot(o, perm[...], preferred_element_type=jnp.float32).astype(jnp.bfloat16)
            for nb in range(4):
                rhs = jnp.concatenate(
                    [wg[:, cc, i, b].reshape(256, 128) for b in (2 * nb, 2 * nb + 1)], axis=1
                )
                at = slice(nb * 256, nb * 256 + 256)
                oacc[:, at] = oacc[:, at] + jnp.dot(o, rhs, preferred_element_type=jnp.float32)
        return 0

    lax.fori_loop(0, 4, project, 0)
    out[...] = oacc[...].astype(jnp.bfloat16)

    for cp in sends:
        cp.wait_send()
    for t in range(8):
        relay_sent(t, slots[t])
    for d in range(4):
        given(d)


def body(queries, keys, values, master, moment, second, gradient):
    bf, f32 = jnp.bfloat16, jnp.float32
    dma = pltpu.SemaphoreType.DMA
    any_ = pl.BlockSpec(memory_space=pl.ANY)
    vmem = pl.BlockSpec(memory_space=pltpu.VMEM)
    projected, new_master = pl.pallas_call(
        kernel,
        name="attn_step",
        out_shape=(
            jax.ShapeDtypeStruct((128, 1024), bf),
            jax.ShapeDtypeStruct((2, 1024), f32),
        ),
        in_specs=[any_] * 3 + [vmem] * 4,
        out_specs=(vmem, vmem),
        scratch_shapes=[
            pltpu.VMEM((8, 128, 256), bf),
            pltpu.VMEM((2, 8, 128, 256), bf),
            pltpu.VMEM((2, 8, 128, 256), bf),
            pltpu.VMEM((2, 4, 256, 256), f32),
            pltpu.VMEM((2, 4, 256, 128), f32),
            pltpu.VMEM((4, 2, 128, 256), bf),
            pltpu.VMEM((8, 128, 256), bf),
            pltpu.VMEM((128, 1024), f32),
            pltpu.VMEM((16, 2, 4, 8, 16, 128), bf),
            pltpu.VMEM((8, 2, 128), f32),
            pltpu.VMEM((8, 2, 128), f32),
            pltpu.VMEM((16, 128), f32),
            pltpu.VMEM((256, 256), bf),
            dma((7,)), dma((8,)), dma((7,)), dma((8,)), dma((7,)), dma((8,)),
            dma((8,)), dma((8,)), dma((8,)), dma((8,)),
            dma((8,)), dma((8,)), dma((8,)), dma((8,)), dma((4,)), dma((4,)),
            dma((8, 4)), dma((8, 4)), dma((7, 4)), dma((7, 4)),
            dma((1,)), dma((1,)), dma((8,)), dma((8,)), dma((7,)), dma((7,)),
            dma((4, 2)), dma((8,)),
        ],
        compiler_params=pltpu.CompilerParams(collective_id=1, has_side_effects=True),
    )(queries, keys, values, master, moment, second, gradient)
    return projected[None], new_master


def solution(mesh):
    torus = Mesh(mesh.devices.reshape(SIZES), AXES)
    tokens = P(("l", "z"), ("x", "h", "c"), None)
    rows = P(AXES, None)
    return jax.shard_map(
        body,
        mesh=torus,
        in_specs=(tokens,) * 3 + (rows,) * 4,
        out_specs=(tokens, rows),
        check_vma=False,
    )
```

```python
import math

import jax
import jax.numpy as jnp
from jax import lax
from jax.experimental import pallas as pl
from jax.experimental.pallas import tpu as pltpu
from jax.sharding import Mesh
from jax.sharding import PartitionSpec as P

MESH = pl.DeviceIdType.MESH
AXES = ("x", "h", "c", "l", "z")
SIZES = (4, 2, 2, 4, 16)
HEAD_DIM = 128
SCALE = math.log2(math.e) / math.sqrt(HEAD_DIM)

beta_first = 0.9
beta_second = 0.999
learning_rate = 0.1
weight_decay = 0.1
epsilon = 1e-08
step_count = 10.0


def adamw(master, moment, second, gradient):
    moment_new = beta_first * moment + (1.0 - beta_first) * gradient
    second_new = beta_second * second + (1.0 - beta_second) * gradient * gradient
    moment_hat = moment_new / (1.0 - beta_first**step_count)
    second_hat = second_new / (1.0 - beta_second**step_count)
    return master - learning_rate * (
        moment_hat / (jnp.sqrt(second_hat) + epsilon) + weight_decay * master
    )


def kernel(
    q_in, k_in, v_in, ma, mo, se, gr,
    out, nm_out,
    qb, kb, vb, acc, mx, osrc, ob, oacc, wg, wsrc, wrecv, wasm, perm,
    qs, qr, ks, kr, vs, vr, yks, ykr, yvs, yvr,
    w1s, w1r, w2s, w2r, w3s, w3r, zps, zpr, zms, zmr, sos, sor, sps, spr, sms, smr,
    os, orr,
):
    x, h, c, l, z = (lax.axis_index(a) for a in AXES)
    slot = x * 2 + c
    y = h * 4 + l
    odd = z % 2

    def dev(**kw):
        d = {"x": x, "h": h, "c": c, "l": l, "z": z}
        d.update(kw)
        return d

    def half_peer(k):
        p = (slot + k) % 8
        return p, dev(x=p // 2, c=p % 2)

    def chip_peer(dx, dc):
        px, pc = (x + dx) % 4, (c + dc) % 2
        return px * 2 + pc, dev(x=px, c=pc)

    def y_peer(dy):
        p = (y + dy) % 8
        return p, dev(h=p // 4, l=p % 4)

    partner = dev(h=1 - h)
    sibling = dev(c=1 - c)
    z_next = dev(z=(z + 1) % 16)
    z_prev = dev(z=(z + 15) % 16)

    def remote(src, dst, ss, rs, to):
        return pltpu.make_async_remote_copy(
            src_ref=src, dst_ref=dst, send_sem=ss, recv_sem=rs, device_id=to, device_id_type=MESH
        )

    def landed(ref, sem):
        pltpu.make_async_copy(ref, ref, sem).wait()

    barrier = pltpu.get_barrier_semaphore()
    greeted = [y_peer(d)[1] for d in range(1, 8)]
    greeted += [half_peer(d)[1] for d in range(1, 8)]
    for to in greeted:
        pl.semaphore_signal(barrier, inc=1, device_id=to, device_id_type=MESH)

    new_master = adamw(ma[...], mo[...], se[...], gr[...])
    nm_out[...] = new_master
    for b in range(8):
        wsrc[b] = new_master[:, b * 128 : (b + 1) * 128]

    pl.semaphore_wait(barrier, len(greeted) + 2 * odd)
    for to in (z_next, z_prev):
        pl.semaphore_signal(barrier, inc=1, device_id=to, device_id_type=MESH)

    sends = []

    def start(cp):
        cp.start()
        sends.append(cp)

    order = [(0, 1)] + [(dx, dc) for dc in (0, 1) for dx in (3, 1)] + [(2, 0), (2, 1)]

    def cols(p):
        return pl.ds(pl.multiple_of(p * 256, 256), 256)

    pltpu.make_async_copy(k_in.at[0, :, cols(slot)], kb.at[h, slot], kr.at[slot]).start()
    pltpu.make_async_copy(v_in.at[0, :, cols(slot)], vb.at[h, slot], vr.at[slot]).start()
    pltpu.make_async_copy(wsrc.at[y], wrecv.at[y], w1r.at[y]).start()
    for d in range(1, 8):
        p, to = y_peer(d)
        start(remote(wsrc.at[p], wrecv.at[y], w1s.at[d], w1r.at[y], to))
    for n, (dx, dc) in enumerate(order):
        p, to = chip_peer(dx, dc)
        start(remote(k_in.at[0, :, cols(p)], kb.at[h, slot], ks.at[n], kr.at[slot], to))
        start(remote(v_in.at[0, :, cols(p)], vb.at[h, slot], vs.at[n], vr.at[slot], to))

    def relay(t, j):
        landed(kb.at[h, j], kr.at[j])
        landed(vb.at[h, j], vr.at[j])

        @pl.when(jnp.logical_or(h == 0, j < 6))
        def _():
            remote(kb.at[h, j], kb.at[h, j], yks.at[t], ykr.at[j], partner).start()
            remote(vb.at[h, j], vb.at[h, j], yvs.at[t], yvr.at[j], partner).start()

    def relay_sent(t, j):
        @pl.when(jnp.logical_or(h == 0, j < 6))
        def _():
            remote(kb.at[h, j], kb.at[h, j], yks.at[t], ykr.at[j], partner).wait_send()
            remote(vb.at[h, j], vb.at[h, j], yvs.at[t], yvr.at[j], partner).wait_send()

    slots = [slot, x * 2 + (1 - c)]
    for t in range(3):
        g = jnp.where(t >= x, t + 1, t)
        slots += [2 * g, 2 * g + 1]

    relay(0, slots[0])
    relay(1, slots[1])

    for i in range(8):
        landed(wrecv.at[i], w1r.at[i])
    for i in range(8):
        wasm[2 * i : 2 * i + 2, :] = wrecv[i]
    wg[z, c, x, y] = wasm[...].astype(jnp.bfloat16)

    for d in range(1, 8):
        p, to = y_peer(d)
        start(remote(wg.at[z, c, x, y], wg.at[z, c, x, y], w2s.at[d], w2r.at[y], to))

    to_col = lax.broadcasted_iota(jnp.int32, (256, 256), 1)
    from_row = lax.broadcasted_iota(jnp.int32, (256, 256), 0)
    wanted = (
        ((to_col >> 3) & 1) * 128 + ((to_col >> 1) & 3) * 32 + (to_col >> 4) * 2 + (to_col & 1)
    )
    perm[...] = jnp.where(from_row == wanted, 1.0, 0.0).astype(jnp.bfloat16)

    for d in range(1, 8):
        p = (y + d) % 8
        landed(wg.at[z, c, x, p], w2r.at[p])
    for d in range(1, 4):
        px = (x + d) % 4
        start(remote(wg.at[z, c, x], wg.at[z, c, x], w3s.at[d], w3r.at[x], dev(x=px)))

    pltpu.make_async_copy(q_in.at[0, :, cols(slot)], qb.at[slot], qr.at[slot]).start()
    for n, (dx, dc) in enumerate(order):
        p, to = chip_peer(dx, dc)
        start(remote(q_in.at[0, :, cols(p)], qb.at[slot], qs.at[n], qr.at[slot], to))

    for t in range(2, 8):
        relay(t, slots[t])

    for d in range(1, 4):
        px = (x + d) % 4
        landed(wg.at[z, c, px], w3r.at[px])

    def part(zc, u):
        return wg.at[zc, c, u]

    @pl.when(odd == 0)
    def _():
        pl.semaphore_wait(barrier, 2)

    for u in range(4):
        start(remote(part(z, u), part(z, u), zps.at[0, u], zpr.at[0, u], z_next))
        start(remote(part(z, u), part(z, u), zms.at[0, u], zmr.at[0, u], z_prev))
    start(remote(wg.at[z, c], wg.at[z, c], sos.at[0], sor.at[0], sibling))

    def onward(t, u):
        zp = (z + 16 - t) % 16
        zm = (z + t) % 16
        up = remote(part(zp, u), part(zp, u), zps.at[t, u], zpr.at[t, u], z_next)
        if t == 7:
            return up, None
        return up, remote(part(zm, u), part(zm, u), zms.at[t, u], zmr.at[t, u], z_prev)

    def across(t):
        zp = (z + 15 - t) % 16
        zm = (z + 1 + t) % 16
        both = [remote(wg.at[zp, c], wg.at[zp, c], sps.at[t], spr.at[t], sibling)]
        if t < 7:
            both.append(remote(wg.at[zm, c], wg.at[zm, c], sms.at[t], smr.at[t], sibling))
        return both

    def ring(t):
        zp = (z + 15 - t) % 16
        zm = (z + 1 + t) % 16
        for u in range(4):
            landed(part(zp, u), zpr.at[t, u])
            if t < 7:
                up, down = onward(t + 1, u)
                up.start()
                landed(part(zm, u), zmr.at[t, u])
                if down is not None:
                    down.start()
        for cp in across(t):
            cp.start()

    def ring_sent():
        for t in range(8):
            for cp in across(t):
                cp.wait_send()
            if t > 0:
                for u in range(4):
                    for cp in onward(t, u):
                        if cp is not None:
                            cp.wait_send()

    def attend(qg, kh, kg, diagonal):
        for hh in range(2):
            lanes = slice(hh * 128, hh * 128 + 128)
            q = qb[pl.ds(2 * qg, 2), :, lanes].reshape(256, 128)
            k = kb[kh, pl.ds(2 * kg, 2), :, lanes].reshape(256, 128)
            v = vb[kh, pl.ds(2 * kg, 2), :, lanes].reshape(256, 128)
            s = lax.dot_general(q, k, (((1,), (1,)), ((), ())), preferred_element_type=jnp.float32)
            s = s * SCALE
            if diagonal:
                rows = lax.broadcasted_iota(jnp.int32, (256, 256), 0)
                keys = lax.broadcasted_iota(jnp.int32, (256, 256), 1)
                s = jnp.where(rows >= keys, s, -jnp.inf)
            top = jnp.broadcast_to(jnp.max(s, axis=1, keepdims=True), (256, 128))
            v1 = jnp.concatenate([v, jnp.ones((256, 128), jnp.bfloat16)], axis=1)
            if diagonal:
                new = top
            else:
                old = mx[hh, qg]
                new = jnp.maximum(old, top)
            p = jnp.exp2(s - jnp.concatenate([new, new], axis=1)).astype(jnp.bfloat16)
            pv = jnp.dot(p, v1, preferred_element_type=jnp.float32)
            if diagonal:
                acc[hh, qg] = pv
            else:
                fade = jnp.exp2(old - new)
                acc[hh, qg] = acc[hh, qg] * jnp.concatenate([fade, fade], axis=1) + pv
            mx[hh, qg] = new

    def own(qg):
        attend(qg, h, qg, True)

        def step(g, _):
            attend(qg, h, g, False)
            return 0

        lax.fori_loop(0, qg, step, 0)

    def give(d):
        for hh in range(2):
            total = acc[hh, d]
            o = (total[:, :128] / total[:, 128:]).astype(jnp.bfloat16)
            for cc in range(2):
                osrc[d, cc, :, hh * 128 : hh * 128 + 128] = o[cc * 128 : cc * 128 + 128]
        for cc in range(2):
            self_ = jnp.logical_and(d == x, cc == c)

            @pl.when(self_)
            def _():
                pltpu.make_async_copy(osrc.at[d, cc], ob.at[slot], orr.at[slot]).start()

            @pl.when(jnp.logical_not(self_))
            def _():
                remote(osrc.at[d, cc], ob.at[slot], os.at[d, cc], orr.at[slot], dev(x=d, c=cc)).start()

    def given(d):
        for cc in range(2):
            @pl.when(jnp.logical_not(jnp.logical_and(d == x, cc == c)))
            def _():
                remote(osrc.at[d, cc], ob.at[slot], os.at[d, cc], orr.at[slot], dev(x=d, c=cc)).wait_send()

    def cross(g):
        for j in (2 * g, 2 * g + 1):
            landed(kb.at[1 - h, j], ykr.at[j])
            landed(vb.at[1 - h, j], yvr.at[j])

        def step(qg, _):
            attend(qg, 1 - h, g, False)
            return 0

        lax.fori_loop(g + 1 - h, 4, step, 0)

    for j in range(8):
        landed(qb.at[j], qr.at[j])
    def first():
        own(0)

        @pl.when(h == 0)
        def _():
            give(0)

    def meet(g):
        if g < 3:
            cross(g)
            give(g + 1 - h)
        else:

            @pl.when(h == 1)
            def _():
                cross(3)
                give(3)

    def run(*steps):
        for f, t in steps:
            f(t)

    first()

    @pl.when(z >= 8)
    def _():
        run(
            (ring, 0), (own, 1), (ring, 1), (own, 2), (ring, 2), (own, 3),
            (ring, 3), (ring, 4), (ring, 5), (ring, 6), (ring, 7),
            (meet, 0), (meet, 1), (meet, 2), (meet, 3),
        )

    @pl.when(jnp.logical_and(z >= 4, z < 8))
    def _():
        run(
            (ring, 0), (own, 1), (ring, 1), (own, 2), (ring, 2), (own, 3),
            (ring, 3), (ring, 4), (ring, 5), (meet, 0), (meet, 1), (meet, 2),
            (ring, 6), (ring, 7), (meet, 3),
        )

    @pl.when(z < 4)
    def _():
        run(
            (own, 1), (own, 2), (own, 3), (ring, 0), (meet, 0), (ring, 1), (meet, 1),
            (ring, 2), (ring, 3), (meet, 2), (ring, 4), (ring, 5), (meet, 3), (ring, 6), (ring, 7),
        )

    landed(wg.at[z, 1 - c], sor.at[0])
    for t in range(8):
        landed(wg.at[(z + 15 - t) % 16, 1 - c], spr.at[t])
    for t in range(7):
        landed(wg.at[(z + 1 + t) % 16, 1 - c], smr.at[t])

    oacc[...] = jnp.zeros((128, 1024), jnp.float32)

    def project(i, _):
        landed(ob.at[2 * i], orr.at[2 * i])
        landed(ob.at[2 * i + 1], orr.at[2 * i + 1])
        for cc in range(2):
            lanes = slice(cc * 128, cc * 128 + 128)
            o = jnp.concatenate([ob[2 * i, :, lanes], ob[2 * i + 1, :, lanes]], axis=1)
            o = jnp.dot(o, perm[...], preferred_element_type=jnp.float32).astype(jnp.bfloat16)
            for nb in range(4):
                rhs = jnp.concatenate(
                    [wg[:, cc, i, b].reshape(256, 128) for b in (2 * nb, 2 * nb + 1)], axis=1
                )
                at = slice(nb * 256, nb * 256 + 256)
                oacc[:, at] = oacc[:, at] + jnp.dot(o, rhs, preferred_element_type=jnp.float32)
        return 0

    lax.fori_loop(0, 4, project, 0)
    out[...] = oacc[...].astype(jnp.bfloat16)

    for cp in sends:
        cp.wait_send()
    ring_sent()
    for t in range(8):
        relay_sent(t, slots[t])
    for d in range(4):
        given(d)


def body(queries, keys, values, master, moment, second, gradient):
    bf, f32 = jnp.bfloat16, jnp.float32
    dma = pltpu.SemaphoreType.DMA
    any_ = pl.BlockSpec(memory_space=pl.ANY)
    vmem = pl.BlockSpec(memory_space=pltpu.VMEM)
    projected, new_master = pl.pallas_call(
        kernel,
        name="attn_step",
        out_shape=(
            jax.ShapeDtypeStruct((128, 1024), bf),
            jax.ShapeDtypeStruct((2, 1024), f32),
        ),
        in_specs=[any_] * 3 + [vmem] * 4,
        out_specs=(vmem, vmem),
        scratch_shapes=[
            pltpu.VMEM((8, 128, 256), bf),
            pltpu.VMEM((2, 8, 128, 256), bf),
            pltpu.VMEM((2, 8, 128, 256), bf),
            pltpu.VMEM((2, 4, 256, 256), f32),
            pltpu.VMEM((2, 4, 256, 128), f32),
            pltpu.VMEM((4, 2, 128, 256), bf),
            pltpu.VMEM((8, 128, 256), bf),
            pltpu.VMEM((128, 1024), f32),
            pltpu.VMEM((16, 2, 4, 8, 16, 128), bf),
            pltpu.VMEM((8, 2, 128), f32),
            pltpu.VMEM((8, 2, 128), f32),
            pltpu.VMEM((16, 128), f32),
            pltpu.VMEM((256, 256), bf),
            dma((7,)), dma((8,)), dma((7,)), dma((8,)), dma((7,)), dma((8,)),
            dma((8,)), dma((8,)), dma((8,)), dma((8,)),
            dma((8,)), dma((8,)), dma((8,)), dma((8,)), dma((4,)), dma((4,)),
            dma((8, 4)), dma((8, 4)), dma((7, 4)), dma((7, 4)),
            dma((1,)), dma((1,)), dma((8,)), dma((8,)), dma((7,)), dma((7,)),
            dma((4, 2)), dma((8,)),
        ],
        compiler_params=pltpu.CompilerParams(collective_id=1, has_side_effects=True),
    )(queries, keys, values, master, moment, second, gradient)
    return projected[None], new_master


def solution(mesh):
    torus = Mesh(mesh.devices.reshape(SIZES), AXES)
    tokens = P(("l", "z"), ("x", "h", "c"), None)
    rows = P(AXES, None)
    return jax.shard_map(
        body,
        mesh=torus,
        in_specs=(tokens,) * 3 + (rows,) * 4,
        out_specs=(tokens, rows),
        check_vma=False,
    )
```

```python
import math

import jax
import jax.numpy as jnp
from jax import lax
from jax.experimental import pallas as pl
from jax.experimental.pallas import tpu as pltpu
from jax.sharding import Mesh
from jax.sharding import PartitionSpec as P

MESH = pl.DeviceIdType.MESH
AXES = ("x", "h", "c", "l", "z")
SIZES = (4, 2, 2, 4, 16)
HEAD_DIM = 128
SCALE = math.log2(math.e) / math.sqrt(HEAD_DIM)

beta_first = 0.9
beta_second = 0.999
learning_rate = 0.1
weight_decay = 0.1
epsilon = 1e-08
step_count = 10.0


def adamw(master, moment, second, gradient):
    moment_new = beta_first * moment + (1.0 - beta_first) * gradient
    second_new = beta_second * second + (1.0 - beta_second) * gradient * gradient
    moment_hat = moment_new / (1.0 - beta_first**step_count)
    second_hat = second_new / (1.0 - beta_second**step_count)
    return master - learning_rate * (
        moment_hat / (jnp.sqrt(second_hat) + epsilon) + weight_decay * master
    )


def kernel(
    q_in, k_in, v_in, ma, mo, se, gr,
    out, nm_out,
    qb, kb, vb, acc, mx, osrc, ob, oacc, wg, wsrc, wrecv, wasm, perm,
    qs, qr, ks, kr, vs, vr, yks, ykr, yvs, yvr,
    w1s, w1r, w2s, w2r, w3s, w3r, zps, zpr, zms, zmr, sos, sor, sps, spr, sms, smr,
    os, orr,
):
    x, h, c, l, z = (lax.axis_index(a) for a in AXES)
    slot = x * 2 + c
    y = h * 4 + l
    odd = z % 2

    def dev(**kw):
        d = {"x": x, "h": h, "c": c, "l": l, "z": z}
        d.update(kw)
        return d

    def half_peer(k):
        p = (slot + k) % 8
        return p, dev(x=p // 2, c=p % 2)

    def chip_peer(dx, dc):
        px, pc = (x + dx) % 4, (c + dc) % 2
        return px * 2 + pc, dev(x=px, c=pc)

    def y_peer(dy):
        p = (y + dy) % 8
        return p, dev(h=p // 4, l=p % 4)

    partner = dev(h=1 - h)
    sibling = dev(c=1 - c)
    z_next = dev(z=(z + 1) % 16)
    z_prev = dev(z=(z + 15) % 16)

    def remote(src, dst, ss, rs, to):
        return pltpu.make_async_remote_copy(
            src_ref=src, dst_ref=dst, send_sem=ss, recv_sem=rs, device_id=to, device_id_type=MESH
        )

    def landed(ref, sem):
        pltpu.make_async_copy(ref, ref, sem).wait()

    barrier = pltpu.get_barrier_semaphore()
    greeted = [y_peer(d)[1] for d in range(1, 8)]
    greeted += [half_peer(d)[1] for d in range(1, 8)]
    for to in greeted:
        pl.semaphore_signal(barrier, inc=1, device_id=to, device_id_type=MESH)

    new_master = adamw(ma[...], mo[...], se[...], gr[...])
    nm_out[...] = new_master
    for b in range(8):
        wsrc[b] = new_master[:, b * 128 : (b + 1) * 128]

    pl.semaphore_wait(barrier, len(greeted) + 2 * odd)
    for to in (z_next, z_prev):
        pl.semaphore_signal(barrier, inc=1, device_id=to, device_id_type=MESH)

    sends = []

    def start(cp):
        cp.start()
        sends.append(cp)

    order = [(0, 1)] + [(dx, dc) for dc in (0, 1) for dx in (3, 1)] + [(2, 0), (2, 1)]

    def cols(p):
        return pl.ds(pl.multiple_of(p * 256, 256), 256)

    pltpu.make_async_copy(k_in.at[0, :, cols(slot)], kb.at[h, slot], kr.at[slot]).start()
    pltpu.make_async_copy(v_in.at[0, :, cols(slot)], vb.at[h, slot], vr.at[slot]).start()
    pltpu.make_async_copy(wsrc.at[y], wrecv.at[y], w1r.at[y]).start()
    for d in range(1, 8):
        p, to = y_peer(d)
        start(remote(wsrc.at[p], wrecv.at[y], w1s.at[d], w1r.at[y], to))
    for n, (dx, dc) in enumerate(order):
        p, to = chip_peer(dx, dc)
        start(remote(k_in.at[0, :, cols(p)], kb.at[h, slot], ks.at[n], kr.at[slot], to))
        start(remote(v_in.at[0, :, cols(p)], vb.at[h, slot], vs.at[n], vr.at[slot], to))

    def relay(t, j):
        landed(kb.at[h, j], kr.at[j])
        landed(vb.at[h, j], vr.at[j])

        @pl.when(jnp.logical_or(h == 0, j < 6))
        def _():
            remote(kb.at[h, j], kb.at[h, j], yks.at[t], ykr.at[j], partner).start()
            remote(vb.at[h, j], vb.at[h, j], yvs.at[t], yvr.at[j], partner).start()

    def relay_sent(t, j):
        @pl.when(jnp.logical_or(h == 0, j < 6))
        def _():
            remote(kb.at[h, j], kb.at[h, j], yks.at[t], ykr.at[j], partner).wait_send()
            remote(vb.at[h, j], vb.at[h, j], yvs.at[t], yvr.at[j], partner).wait_send()

    slots = [slot, x * 2 + (1 - c)]
    for t in range(3):
        g = jnp.where(t >= x, t + 1, t)
        slots += [2 * g, 2 * g + 1]

    for i in range(8):
        landed(wrecv.at[i], w1r.at[i])
    for i in range(8):
        wasm[2 * i : 2 * i + 2, :] = wrecv[i]
    wg[z, c, x, y] = wasm[...].astype(jnp.bfloat16)

    for d in range(1, 8):
        p, to = y_peer(d)
        start(remote(wg.at[z, c, x, y], wg.at[z, c, x, y], w2s.at[d], w2r.at[y], to))

    relay(0, slots[0])
    relay(1, slots[1])

    to_col = lax.broadcasted_iota(jnp.int32, (256, 256), 1)
    from_row = lax.broadcasted_iota(jnp.int32, (256, 256), 0)
    wanted = (
        ((to_col >> 3) & 1) * 128 + ((to_col >> 1) & 3) * 32 + (to_col >> 4) * 2 + (to_col & 1)
    )
    perm[...] = jnp.where(from_row == wanted, 1.0, 0.0).astype(jnp.bfloat16)

    for d in range(1, 8):
        p = (y + d) % 8
        landed(wg.at[z, c, x, p], w2r.at[p])
    for d in range(1, 4):
        px = (x + d) % 4
        start(remote(wg.at[z, c, x], wg.at[z, c, x], w3s.at[d], w3r.at[x], dev(x=px)))

    pltpu.make_async_copy(q_in.at[0, :, cols(slot)], qb.at[slot], qr.at[slot]).start()
    for n, (dx, dc) in enumerate(order):
        p, to = chip_peer(dx, dc)
        start(remote(q_in.at[0, :, cols(p)], qb.at[slot], qs.at[n], qr.at[slot], to))

    for t in range(2, 8):
        relay(t, slots[t])

    for d in range(1, 4):
        px = (x + d) % 4
        landed(wg.at[z, c, px], w3r.at[px])

    def part(zc, u):
        return wg.at[zc, c, u]

    @pl.when(odd == 0)
    def _():
        pl.semaphore_wait(barrier, 2)

    for u in range(4):
        start(remote(part(z, u), part(z, u), zps.at[0, u], zpr.at[0, u], z_next))
        start(remote(part(z, u), part(z, u), zms.at[0, u], zmr.at[0, u], z_prev))
    start(remote(wg.at[z, c], wg.at[z, c], sos.at[0], sor.at[0], sibling))

    def onward(t, u):
        zp = (z + 16 - t) % 16
        zm = (z + t) % 16
        up = remote(part(zp, u), part(zp, u), zps.at[t, u], zpr.at[t, u], z_next)
        if t == 7:
            return up, None
        return up, remote(part(zm, u), part(zm, u), zms.at[t, u], zmr.at[t, u], z_prev)

    def across(t):
        zp = (z + 15 - t) % 16
        zm = (z + 1 + t) % 16
        both = [remote(wg.at[zp, c], wg.at[zp, c], sps.at[t], spr.at[t], sibling)]
        if t < 7:
            both.append(remote(wg.at[zm, c], wg.at[zm, c], sms.at[t], smr.at[t], sibling))
        return both

    def ring(t):
        zp = (z + 15 - t) % 16
        zm = (z + 1 + t) % 16
        for u in range(4):
            landed(part(zp, u), zpr.at[t, u])
            if t < 7:
                up, down = onward(t + 1, u)
                up.start()
                landed(part(zm, u), zmr.at[t, u])
                if down is not None:
                    down.start()
        for cp in across(t):
            cp.start()

    def ring_sent():
        for t in range(8):
            for cp in across(t):
                cp.wait_send()
            if t > 0:
                for u in range(4):
                    for cp in onward(t, u):
                        if cp is not None:
                            cp.wait_send()

    def attend(qg, kh, kg, diagonal):
        for hh in range(2):
            lanes = slice(hh * 128, hh * 128 + 128)
            q = qb[pl.ds(2 * qg, 2), :, lanes].reshape(256, 128)
            k = kb[kh, pl.ds(2 * kg, 2), :, lanes].reshape(256, 128)
            v = vb[kh, pl.ds(2 * kg, 2), :, lanes].reshape(256, 128)
            s = lax.dot_general(q, k, (((1,), (1,)), ((), ())), preferred_element_type=jnp.float32)
            s = s * SCALE
            if diagonal:
                rows = lax.broadcasted_iota(jnp.int32, (256, 256), 0)
                keys = lax.broadcasted_iota(jnp.int32, (256, 256), 1)
                s = jnp.where(rows >= keys, s, -jnp.inf)
            top = jnp.broadcast_to(jnp.max(s, axis=1, keepdims=True), (256, 128))
            v1 = jnp.concatenate([v, jnp.ones((256, 128), jnp.bfloat16)], axis=1)
            if diagonal:
                new = top
            else:
                old = mx[hh, qg]
                new = jnp.maximum(old, top)
            p = jnp.exp2(s - jnp.concatenate([new, new], axis=1)).astype(jnp.bfloat16)
            pv = jnp.dot(p, v1, preferred_element_type=jnp.float32)
            if diagonal:
                acc[hh, qg] = pv
            else:
                fade = jnp.exp2(old - new)
                acc[hh, qg] = acc[hh, qg] * jnp.concatenate([fade, fade], axis=1) + pv
            mx[hh, qg] = new

    def own(qg):
        attend(qg, h, qg, True)

        def step(g, _):
            attend(qg, h, g, False)
            return 0

        lax.fori_loop(0, qg, step, 0)

    def give(d):
        for hh in range(2):
            total = acc[hh, d]
            o = (total[:, :128] / total[:, 128:]).astype(jnp.bfloat16)
            for cc in range(2):
                osrc[d, cc, :, hh * 128 : hh * 128 + 128] = o[cc * 128 : cc * 128 + 128]
        for cc in range(2):
            self_ = jnp.logical_and(d == x, cc == c)

            @pl.when(self_)
            def _():
                pltpu.make_async_copy(osrc.at[d, cc], ob.at[slot], orr.at[slot]).start()

            @pl.when(jnp.logical_not(self_))
            def _():
                remote(osrc.at[d, cc], ob.at[slot], os.at[d, cc], orr.at[slot], dev(x=d, c=cc)).start()

    def given(d):
        for cc in range(2):
            @pl.when(jnp.logical_not(jnp.logical_and(d == x, cc == c)))
            def _():
                remote(osrc.at[d, cc], ob.at[slot], os.at[d, cc], orr.at[slot], dev(x=d, c=cc)).wait_send()

    def cross(g):
        for j in (2 * g, 2 * g + 1):
            landed(kb.at[1 - h, j], ykr.at[j])
            landed(vb.at[1 - h, j], yvr.at[j])

        def step(qg, _):
            attend(qg, 1 - h, g, False)
            return 0

        lax.fori_loop(g + 1 - h, 4, step, 0)

    for j in range(8):
        landed(qb.at[j], qr.at[j])
    def first():
        own(0)

        @pl.when(h == 0)
        def _():
            give(0)

    def meet(g):
        if g < 3:
            cross(g)
            give(g + 1 - h)
        else:

            @pl.when(h == 1)
            def _():
                cross(3)
                give(3)

    def run(*steps):
        for f, t in steps:
            f(t)

    first()

    @pl.when(z >= 8)
    def _():
        run(
            (ring, 0), (own, 1), (ring, 1), (own, 2), (ring, 2), (own, 3),
            (ring, 3), (ring, 4), (ring, 5), (ring, 6), (ring, 7),
            (meet, 0), (meet, 1), (meet, 2), (meet, 3),
        )

    @pl.when(jnp.logical_and(z >= 4, z < 8))
    def _():
        run(
            (ring, 0), (own, 1), (ring, 1), (own, 2), (ring, 2), (own, 3),
            (ring, 3), (ring, 4), (ring, 5), (meet, 0), (meet, 1), (meet, 2),
            (ring, 6), (ring, 7), (meet, 3),
        )

    @pl.when(z < 4)
    def _():
        run(
            (own, 1), (own, 2), (own, 3), (ring, 0), (meet, 0), (ring, 1), (meet, 1),
            (ring, 2), (ring, 3), (meet, 2), (ring, 4), (ring, 5), (meet, 3), (ring, 6), (ring, 7),
        )

    landed(wg.at[z, 1 - c], sor.at[0])
    for t in range(8):
        landed(wg.at[(z + 15 - t) % 16, 1 - c], spr.at[t])
    for t in range(7):
        landed(wg.at[(z + 1 + t) % 16, 1 - c], smr.at[t])

    oacc[...] = jnp.zeros((128, 1024), jnp.float32)

    def project(i, _):
        landed(ob.at[2 * i], orr.at[2 * i])
        landed(ob.at[2 * i + 1], orr.at[2 * i + 1])
        for cc in range(2):
            lanes = slice(cc * 128, cc * 128 + 128)
            o = jnp.concatenate([ob[2 * i, :, lanes], ob[2 * i + 1, :, lanes]], axis=1)
            o = jnp.dot(o, perm[...], preferred_element_type=jnp.float32).astype(jnp.bfloat16)
            for nb in range(4):
                rhs = jnp.concatenate(
                    [wg[:, cc, i, b].reshape(256, 128) for b in (2 * nb, 2 * nb + 1)], axis=1
                )
                at = slice(nb * 256, nb * 256 + 256)
                oacc[:, at] = oacc[:, at] + jnp.dot(o, rhs, preferred_element_type=jnp.float32)
        return 0

    lax.fori_loop(0, 4, project, 0)
    out[...] = oacc[...].astype(jnp.bfloat16)

    for cp in sends:
        cp.wait_send()
    ring_sent()
    for t in range(8):
        relay_sent(t, slots[t])
    for d in range(4):
        given(d)


def body(queries, keys, values, master, moment, second, gradient):
    bf, f32 = jnp.bfloat16, jnp.float32
    dma = pltpu.SemaphoreType.DMA
    any_ = pl.BlockSpec(memory_space=pl.ANY)
    vmem = pl.BlockSpec(memory_space=pltpu.VMEM)
    projected, new_master = pl.pallas_call(
        kernel,
        name="attn_step",
        out_shape=(
            jax.ShapeDtypeStruct((128, 1024), bf),
            jax.ShapeDtypeStruct((2, 1024), f32),
        ),
        in_specs=[any_] * 3 + [vmem] * 4,
        out_specs=(vmem, vmem),
        scratch_shapes=[
            pltpu.VMEM((8, 128, 256), bf),
            pltpu.VMEM((2, 8, 128, 256), bf),
            pltpu.VMEM((2, 8, 128, 256), bf),
            pltpu.VMEM((2, 4, 256, 256), f32),
            pltpu.VMEM((2, 4, 256, 128), f32),
            pltpu.VMEM((4, 2, 128, 256), bf),
            pltpu.VMEM((8, 128, 256), bf),
            pltpu.VMEM((128, 1024), f32),
            pltpu.VMEM((16, 2, 4, 8, 16, 128), bf),
            pltpu.VMEM((8, 2, 128), f32),
            pltpu.VMEM((8, 2, 128), f32),
            pltpu.VMEM((16, 128), f32),
            pltpu.VMEM((256, 256), bf),
            dma((7,)), dma((8,)), dma((7,)), dma((8,)), dma((7,)), dma((8,)),
            dma((8,)), dma((8,)), dma((8,)), dma((8,)),
            dma((8,)), dma((8,)), dma((8,)), dma((8,)), dma((4,)), dma((4,)),
            dma((8, 4)), dma((8, 4)), dma((7, 4)), dma((7, 4)),
            dma((1,)), dma((1,)), dma((8,)), dma((8,)), dma((7,)), dma((7,)),
            dma((4, 2)), dma((8,)),
        ],
        compiler_params=pltpu.CompilerParams(collective_id=1, has_side_effects=True),
    )(queries, keys, values, master, moment, second, gradient)
    return projected[None], new_master


def solution(mesh):
    torus = Mesh(mesh.devices.reshape(SIZES), AXES)
    tokens = P(("l", "z"), ("x", "h", "c"), None)
    rows = P(AXES, None)
    return jax.shard_map(
        body,
        mesh=torus,
        in_specs=(tokens,) * 3 + (rows,) * 4,
        out_specs=(tokens, rows),
        check_vma=False,
    )
```

```python
import math

import jax
import jax.numpy as jnp
from jax import lax
from jax.experimental import pallas as pl
from jax.experimental.pallas import tpu as pltpu
from jax.sharding import Mesh
from jax.sharding import PartitionSpec as P

MESH = pl.DeviceIdType.MESH
AXES = ("x", "h", "c", "l", "z")
SIZES = (4, 2, 2, 4, 16)
HEAD_DIM = 128
SCALE = math.log2(math.e) / math.sqrt(HEAD_DIM)

beta_first = 0.9
beta_second = 0.999
learning_rate = 0.1
weight_decay = 0.1
epsilon = 1e-08
step_count = 10.0


def adamw(master, moment, second, gradient):
    moment_new = beta_first * moment + (1.0 - beta_first) * gradient
    second_new = beta_second * second + (1.0 - beta_second) * gradient * gradient
    moment_hat = moment_new / (1.0 - beta_first**step_count)
    second_hat = second_new / (1.0 - beta_second**step_count)
    return master - learning_rate * (
        moment_hat / (jnp.sqrt(second_hat) + epsilon) + weight_decay * master
    )


def kernel(
    q_in, k_in, v_in, ma, mo, se, gr,
    out, nm_out,
    qb, kb, vb, acc, mx, osrc, ob, oacc, wg, wsrc, wrecv, wasm, perm,
    qs, qr, ks, kr, vs, vr, yks, ykr, yvs, yvr,
    w1s, w1r, w2s, w2r, w3s, w3r, zps, zpr, zms, zmr, sos, sor, sps, spr, sms, smr,
    os, orr,
):
    x, h, c, l, z = (lax.axis_index(a) for a in AXES)
    slot = x * 2 + c
    y = h * 4 + l
    odd = z % 2

    def dev(**kw):
        d = {"x": x, "h": h, "c": c, "l": l, "z": z}
        d.update(kw)
        return d

    def half_peer(k):
        p = (slot + k) % 8
        return p, dev(x=p // 2, c=p % 2)

    def chip_peer(dx, dc):
        px, pc = (x + dx) % 4, (c + dc) % 2
        return px * 2 + pc, dev(x=px, c=pc)

    def y_peer(dy):
        p = (y + dy) % 8
        return p, dev(h=p // 4, l=p % 4)

    partner = dev(h=1 - h)
    sibling = dev(c=1 - c)
    z_next = dev(z=(z + 1) % 16)
    z_prev = dev(z=(z + 15) % 16)

    def remote(src, dst, ss, rs, to):
        return pltpu.make_async_remote_copy(
            src_ref=src, dst_ref=dst, send_sem=ss, recv_sem=rs, device_id=to, device_id_type=MESH
        )

    def landed(ref, sem):
        pltpu.make_async_copy(ref, ref, sem).wait()

    barrier = pltpu.get_barrier_semaphore()
    greeted = [y_peer(d)[1] for d in range(1, 8)]
    greeted += [half_peer(d)[1] for d in range(1, 8)]
    for to in greeted:
        pl.semaphore_signal(barrier, inc=1, device_id=to, device_id_type=MESH)

    new_master = adamw(ma[...], mo[...], se[...], gr[...])
    nm_out[...] = new_master
    for b in range(8):
        wsrc[b] = new_master[:, b * 128 : (b + 1) * 128]

    pl.semaphore_wait(barrier, len(greeted) + 2 * odd)
    for to in (z_next, z_prev):
        pl.semaphore_signal(barrier, inc=1, device_id=to, device_id_type=MESH)

    sends = []

    def start(cp):
        cp.start()
        sends.append(cp)

    order = [(0, 1)] + [(dx, dc) for dc in (0, 1) for dx in (3, 1)] + [(2, 0), (2, 1)]

    def cols(p):
        return pl.ds(pl.multiple_of(p * 256, 256), 256)

    pltpu.make_async_copy(k_in.at[0, :, cols(slot)], kb.at[h, slot], kr.at[slot]).start()
    pltpu.make_async_copy(v_in.at[0, :, cols(slot)], vb.at[h, slot], vr.at[slot]).start()
    pltpu.make_async_copy(wsrc.at[y], wrecv.at[y], w1r.at[y]).start()
    for d in range(1, 8):
        p, to = y_peer(d)
        start(remote(wsrc.at[p], wrecv.at[y], w1s.at[d], w1r.at[y], to))
    for n, (dx, dc) in enumerate(order):
        p, to = chip_peer(dx, dc)
        start(remote(k_in.at[0, :, cols(p)], kb.at[h, slot], ks.at[n], kr.at[slot], to))
        start(remote(v_in.at[0, :, cols(p)], vb.at[h, slot], vs.at[n], vr.at[slot], to))

    def relay(t, j):
        landed(kb.at[h, j], kr.at[j])
        landed(vb.at[h, j], vr.at[j])

        @pl.when(jnp.logical_or(h == 0, j < 6))
        def _():
            remote(kb.at[h, j], kb.at[h, j], yks.at[t], ykr.at[j], partner).start()
            remote(vb.at[h, j], vb.at[h, j], yvs.at[t], yvr.at[j], partner).start()

    def relay_sent(t, j):
        @pl.when(jnp.logical_or(h == 0, j < 6))
        def _():
            remote(kb.at[h, j], kb.at[h, j], yks.at[t], ykr.at[j], partner).wait_send()
            remote(vb.at[h, j], vb.at[h, j], yvs.at[t], yvr.at[j], partner).wait_send()

    slots = [slot, x * 2 + (1 - c)]
    for t in range(3):
        g = jnp.where(t >= x, t + 1, t)
        slots += [2 * g, 2 * g + 1]

    for i in range(8):
        landed(wrecv.at[i], w1r.at[i])
    for i in range(8):
        wasm[2 * i : 2 * i + 2, :] = wrecv[i]
    wg[z, c, x, y] = wasm[...].astype(jnp.bfloat16)

    for d in range(1, 8):
        p, to = y_peer(d)
        start(remote(wg.at[z, c, x, y], wg.at[z, c, x, y], w2s.at[d], w2r.at[y], to))

    to_col = lax.broadcasted_iota(jnp.int32, (256, 256), 1)
    from_row = lax.broadcasted_iota(jnp.int32, (256, 256), 0)
    wanted = (
        ((to_col >> 3) & 1) * 128 + ((to_col >> 1) & 3) * 32 + (to_col >> 4) * 2 + (to_col & 1)
    )
    perm[...] = jnp.where(from_row == wanted, 1.0, 0.0).astype(jnp.bfloat16)

    for d in range(1, 8):
        p = (y + d) % 8
        landed(wg.at[z, c, x, p], w2r.at[p])
    for d in range(1, 4):
        px = (x + d) % 4
        start(remote(wg.at[z, c, x], wg.at[z, c, x], w3s.at[d], w3r.at[x], dev(x=px)))

    relay(0, slots[0])
    relay(1, slots[1])

    pltpu.make_async_copy(q_in.at[0, :, cols(slot)], qb.at[slot], qr.at[slot]).start()
    for n, (dx, dc) in enumerate(order):
        p, to = chip_peer(dx, dc)
        start(remote(q_in.at[0, :, cols(p)], qb.at[slot], qs.at[n], qr.at[slot], to))

    for t in range(2, 8):
        relay(t, slots[t])

    for d in range(1, 4):
        px = (x + d) % 4
        landed(wg.at[z, c, px], w3r.at[px])

    def part(zc, u):
        return wg.at[zc, c, u]

    @pl.when(odd == 0)
    def _():
        pl.semaphore_wait(barrier, 2)

    for u in range(4):
        start(remote(part(z, u), part(z, u), zps.at[0, u], zpr.at[0, u], z_next))
        start(remote(part(z, u), part(z, u), zms.at[0, u], zmr.at[0, u], z_prev))
    start(remote(wg.at[z, c], wg.at[z, c], sos.at[0], sor.at[0], sibling))

    def onward(t, u):
        zp = (z + 16 - t) % 16
        zm = (z + t) % 16
        up = remote(part(zp, u), part(zp, u), zps.at[t, u], zpr.at[t, u], z_next)
        if t == 7:
            return up, None
        return up, remote(part(zm, u), part(zm, u), zms.at[t, u], zmr.at[t, u], z_prev)

    def across(t):
        zp = (z + 15 - t) % 16
        zm = (z + 1 + t) % 16
        both = [remote(wg.at[zp, c], wg.at[zp, c], sps.at[t], spr.at[t], sibling)]
        if t < 7:
            both.append(remote(wg.at[zm, c], wg.at[zm, c], sms.at[t], smr.at[t], sibling))
        return both

    def ring(t):
        zp = (z + 15 - t) % 16
        zm = (z + 1 + t) % 16
        for u in range(4):
            landed(part(zp, u), zpr.at[t, u])
            if t < 7:
                up, down = onward(t + 1, u)
                up.start()
                landed(part(zm, u), zmr.at[t, u])
                if down is not None:
                    down.start()
        for cp in across(t):
            cp.start()

    def ring_sent():
        for t in range(8):
            for cp in across(t):
                cp.wait_send()
            if t > 0:
                for u in range(4):
                    for cp in onward(t, u):
                        if cp is not None:
                            cp.wait_send()

    def attend(qg, kh, kg, diagonal):
        for hh in range(2):
            lanes = slice(hh * 128, hh * 128 + 128)
            q = qb[pl.ds(2 * qg, 2), :, lanes].reshape(256, 128)
            k = kb[kh, pl.ds(2 * kg, 2), :, lanes].reshape(256, 128)
            v = vb[kh, pl.ds(2 * kg, 2), :, lanes].reshape(256, 128)
            s = lax.dot_general(q, k, (((1,), (1,)), ((), ())), preferred_element_type=jnp.float32)
            s = s * SCALE
            if diagonal:
                rows = lax.broadcasted_iota(jnp.int32, (256, 256), 0)
                keys = lax.broadcasted_iota(jnp.int32, (256, 256), 1)
                s = jnp.where(rows >= keys, s, -jnp.inf)
            top = jnp.broadcast_to(jnp.max(s, axis=1, keepdims=True), (256, 128))
            v1 = jnp.concatenate([v, jnp.ones((256, 128), jnp.bfloat16)], axis=1)
            if diagonal:
                new = top
            else:
                old = mx[hh, qg]
                new = jnp.maximum(old, top)
            p = jnp.exp2(s - jnp.concatenate([new, new], axis=1)).astype(jnp.bfloat16)
            pv = jnp.dot(p, v1, preferred_element_type=jnp.float32)
            if diagonal:
                acc[hh, qg] = pv
            else:
                fade = jnp.exp2(old - new)
                acc[hh, qg] = acc[hh, qg] * jnp.concatenate([fade, fade], axis=1) + pv
            mx[hh, qg] = new

    def own(qg):
        attend(qg, h, qg, True)

        def step(g, _):
            attend(qg, h, g, False)
            return 0

        lax.fori_loop(0, qg, step, 0)

    def give(d):
        for hh in range(2):
            total = acc[hh, d]
            o = (total[:, :128] / total[:, 128:]).astype(jnp.bfloat16)
            for cc in range(2):
                osrc[d, cc, :, hh * 128 : hh * 128 + 128] = o[cc * 128 : cc * 128 + 128]
        for cc in range(2):
            self_ = jnp.logical_and(d == x, cc == c)

            @pl.when(self_)
            def _():
                pltpu.make_async_copy(osrc.at[d, cc], ob.at[slot], orr.at[slot]).start()

            @pl.when(jnp.logical_not(self_))
            def _():
                remote(osrc.at[d, cc], ob.at[slot], os.at[d, cc], orr.at[slot], dev(x=d, c=cc)).start()

    def given(d):
        for cc in range(2):
            @pl.when(jnp.logical_not(jnp.logical_and(d == x, cc == c)))
            def _():
                remote(osrc.at[d, cc], ob.at[slot], os.at[d, cc], orr.at[slot], dev(x=d, c=cc)).wait_send()

    def cross(g):
        for j in (2 * g, 2 * g + 1):
            landed(kb.at[1 - h, j], ykr.at[j])
            landed(vb.at[1 - h, j], yvr.at[j])

        def step(qg, _):
            attend(qg, 1 - h, g, False)
            return 0

        lax.fori_loop(g + 1 - h, 4, step, 0)

    for j in range(8):
        landed(qb.at[j], qr.at[j])
    def first():
        own(0)

        @pl.when(h == 0)
        def _():
            give(0)

    def meet(g):
        if g < 3:
            cross(g)
            give(g + 1 - h)
        else:

            @pl.when(h == 1)
            def _():
                cross(3)
                give(3)

    def run(*steps):
        for f, t in steps:
            f(t)

    first()

    @pl.when(z >= 8)
    def _():
        run(
            (ring, 0), (own, 1), (ring, 1), (own, 2), (ring, 2), (own, 3),
            (ring, 3), (ring, 4), (ring, 5), (ring, 6), (ring, 7),
            (meet, 0), (meet, 1), (meet, 2), (meet, 3),
        )

    @pl.when(jnp.logical_and(z >= 4, z < 8))
    def _():
        run(
            (ring, 0), (own, 1), (ring, 1), (own, 2), (ring, 2), (own, 3),
            (ring, 3), (ring, 4), (ring, 5), (meet, 0), (meet, 1), (meet, 2),
            (ring, 6), (ring, 7), (meet, 3),
        )

    @pl.when(z < 4)
    def _():
        run(
            (own, 1), (own, 2), (own, 3), (ring, 0), (meet, 0), (ring, 1), (meet, 1),
            (ring, 2), (ring, 3), (meet, 2), (ring, 4), (ring, 5), (meet, 3), (ring, 6), (ring, 7),
        )

    landed(wg.at[z, 1 - c], sor.at[0])
    for t in range(8):
        landed(wg.at[(z + 15 - t) % 16, 1 - c], spr.at[t])
    for t in range(7):
        landed(wg.at[(z + 1 + t) % 16, 1 - c], smr.at[t])

    oacc[...] = jnp.zeros((128, 1024), jnp.float32)

    def project(i, _):
        landed(ob.at[2 * i], orr.at[2 * i])
        landed(ob.at[2 * i + 1], orr.at[2 * i + 1])
        for cc in range(2):
            lanes = slice(cc * 128, cc * 128 + 128)
            o = jnp.concatenate([ob[2 * i, :, lanes], ob[2 * i + 1, :, lanes]], axis=1)
            o = jnp.dot(o, perm[...], preferred_element_type=jnp.float32).astype(jnp.bfloat16)
            for nb in range(4):
                rhs = jnp.concatenate(
                    [wg[:, cc, i, b].reshape(256, 128) for b in (2 * nb, 2 * nb + 1)], axis=1
                )
                at = slice(nb * 256, nb * 256 + 256)
                oacc[:, at] = oacc[:, at] + jnp.dot(o, rhs, preferred_element_type=jnp.float32)
        return 0

    lax.fori_loop(0, 4, project, 0)
    out[...] = oacc[...].astype(jnp.bfloat16)

    for cp in sends:
        cp.wait_send()
    ring_sent()
    for t in range(8):
        relay_sent(t, slots[t])
    for d in range(4):
        given(d)


def body(queries, keys, values, master, moment, second, gradient):
    bf, f32 = jnp.bfloat16, jnp.float32
    dma = pltpu.SemaphoreType.DMA
    any_ = pl.BlockSpec(memory_space=pl.ANY)
    vmem = pl.BlockSpec(memory_space=pltpu.VMEM)
    projected, new_master = pl.pallas_call(
        kernel,
        name="attn_step",
        out_shape=(
            jax.ShapeDtypeStruct((128, 1024), bf),
            jax.ShapeDtypeStruct((2, 1024), f32),
        ),
        in_specs=[any_] * 3 + [vmem] * 4,
        out_specs=(vmem, vmem),
        scratch_shapes=[
            pltpu.VMEM((8, 128, 256), bf),
            pltpu.VMEM((2, 8, 128, 256), bf),
            pltpu.VMEM((2, 8, 128, 256), bf),
            pltpu.VMEM((2, 4, 256, 256), f32),
            pltpu.VMEM((2, 4, 256, 128), f32),
            pltpu.VMEM((4, 2, 128, 256), bf),
            pltpu.VMEM((8, 128, 256), bf),
            pltpu.VMEM((128, 1024), f32),
            pltpu.VMEM((16, 2, 4, 8, 16, 128), bf),
            pltpu.VMEM((8, 2, 128), f32),
            pltpu.VMEM((8, 2, 128), f32),
            pltpu.VMEM((16, 128), f32),
            pltpu.VMEM((256, 256), bf),
            dma((7,)), dma((8,)), dma((7,)), dma((8,)), dma((7,)), dma((8,)),
            dma((8,)), dma((8,)), dma((8,)), dma((8,)),
            dma((8,)), dma((8,)), dma((8,)), dma((8,)), dma((4,)), dma((4,)),
            dma((8, 4)), dma((8, 4)), dma((7, 4)), dma((7, 4)),
            dma((1,)), dma((1,)), dma((8,)), dma((8,)), dma((7,)), dma((7,)),
            dma((4, 2)), dma((8,)),
        ],
        compiler_params=pltpu.CompilerParams(collective_id=1, has_side_effects=True),
    )(queries, keys, values, master, moment, second, gradient)
    return projected[None], new_master


def solution(mesh):
    torus = Mesh(mesh.devices.reshape(SIZES), AXES)
    tokens = P(("l", "z"), ("x", "h", "c"), None)
    rows = P(AXES, None)
    return jax.shard_map(
        body,
        mesh=torus,
        in_specs=(tokens,) * 3 + (rows,) * 4,
        out_specs=(tokens, rows),
        check_vma=False,
    )
```
